256 devices in a mesh: gz: 8 (over z_lo, core), gx: 32 (over x, z_hi, y).
Axes of the slice: x: 4, y: 4, z: 8 (z_hi: 2, z_lo: 4; z = z_hi * 4 + z_lo), core: 2. Of those that a mesh axis runs over, the one named last changes fastest.
Arguments:
- state: float32 [6, 128, 8192], P(None, 'gz', 'gx'), may hold values from -5 to 5, as said below
- state_cot: float32 [6, 128, 8192], P(None, 'gz', 'gx'), may hold values from -6 to 6
- w_in: bfloat16 [128, 12], replicated, may hold values from -1.75 to 1.75
- w_mid: bfloat16 [128, 128], replicated, may hold values from -0.5 to 0.5
- w_out: bfloat16 [6, 128], replicated, may hold values from -0.5 to 0.5
- radiation: float32 [128, 128], replicated, may hold values from -0.5 to 0.5
- fall_rate: float32 [8192], P('gx'), may hold values from 20 to 2000
- active: int32 [8192], P('gx'), may hold values 0 or 1
Outputs:
- new_state: float32 [6, 128, 8192], P(None, 'gz', 'gx')
- state_grad: float32 [6, 128, 8192], P(None, 'gz', 'gx')
- grad_in: float32 [128, 12], replicated
- grad_mid: float32 [128, 128], replicated
- grad_out: float32 [6, 128], replicated
The draws below stay inside these ranges and needn't reach their ends.
Inputs may be any that keep to these rules, and one draw needn't show every extreme that they name: `state`: fields come in the order u, v, w, theta, total water, rain water; rain water lies between 0.05 and 1.
All inputs are finite; a program needn't handle non-finite values. No bound on the sum of `active` on one device may be relied on, other than what follows from the above.
Results may differ from the reference program's by a relative error of at most 0.00045.
The reference program's roundings to bfloat16 on the way (of `features`) count: a program that leaves them out, or rounds other values in their place, can miss the bound.
Values sent between devices are 32-bit elements; how exact they have to be, the bound alone decides.
No kernel may reach another device: no remote copies, remote signals or barrier semaphores. Data moves between devices by JAX's collectives and lax.ppermute only.
A program may use at most 64 MiB of HBM per device.

```python
import math
import jax
import jax.numpy as jnp
from jax import lax

NFIELD = 6
HID = 128
NY = 64
NX = 128
NZ = 128
NCOL = 8192


def draw_state(key, part):
    subkeys = jax.random.split(jax.random.fold_in(key, 17), 3)
    scales = jnp.array([1.0, 1.0, 0.5, 1.0, 1.0], jnp.float32)[:, None, None]
    moving = jnp.clip(jax.random.normal(subkeys[1], (5, NZ, NCOL), jnp.float32), -4.0, 4.0) * scales
    rain_water = jnp.exp(jax.random.uniform(subkeys[2], (NZ, NCOL), jnp.float32, math.log(0.05), 0.0))
    return jnp.concatenate([moving, rain_water[None]], 0)


def set_ends(drawn, own_key, smallest, top_value):
    dims = drawn.shape
    index_at = [jax.random.randint(jax.random.fold_in(own_key, axis), (), 0, dims[axis]) for axis in range(len(dims))]
    drawn = drawn.at[tuple(index_at)].set(smallest)
    longest = dims.index(max(dims))
    index_at[longest] = (index_at[longest] + 1) % dims[longest]
    return drawn.at[tuple(index_at)].set(top_value)


def steps_of(rng, dims, cuts, low, high):
    gain = 1.0
    for dim, blocks in cuts:
        draws = jax.random.uniform(jax.random.fold_in(jax.random.fold_in(rng, 6), dim), (blocks,), jnp.float32, low / len(cuts), high / len(cuts))
        gain = gain * jnp.repeat(jnp.exp(draws), dims[dim] // blocks).reshape((-1,) + (1,) * (len(dims) - 1 - dim))
    return gain


def scatter_about(key, shape, deviation, reach, shards=(), kind=jnp.bfloat16):
    gain = steps_of(key, shape, shards, -0.22, 0.18) if shards else 1.0
    entries = jax.random.normal(key, shape, jnp.float32) * deviation * gain
    return jnp.minimum(jnp.maximum(entries, -reach), reach).astype(kind)


def setup_inputs(seed: int = 0) -> dict:
    key_list = jax.random.split(jax.random.key(seed), 9)
    state = draw_state(jax.random.fold_in(key_list[8], 71), 0)
    state_cot = scatter_about(key_list[1], (NFIELD, NZ, NCOL), 1.0, 6.0, ((1, 8), (2, 32)), jnp.float32)
    w_in = scatter_about(key_list[2], (HID, 2 * NFIELD), (2 * NFIELD) ** -0.5, 1.75)
    w_mid = scatter_about(key_list[3], (HID, HID), HID ** -0.5, 0.5)
    w_out = scatter_about(key_list[4], (NFIELD, HID), HID ** -0.5, 0.5)
    radiation = scatter_about(key_list[5], (NZ, NZ), NZ ** -0.5, 0.5, (), jnp.float32)
    fall_rate = jnp.clip(jnp.exp(math.log(2000.0) - 4.6051702 * jax.random.uniform(key_list[6], (NCOL,), jnp.float32) ** steps_of(key_list[6], (NCOL,), ((0, 32),), -0.2, 0.2)), 20.0, 2000.0)
    active = set_ends((jax.random.randint(key_list[7], (NCOL,), 0, 2) < 1).astype(jnp.int32), jax.random.fold_in(key_list[7], 1), 0, 1)
    return dict(state=state, state_cot=state_cot, w_in=w_in, w_mid=w_mid, w_out=w_out, radiation=radiation, fall_rate=fall_rate, active=active)


DIFFUSION = 0.1
TIME_STEP = 0.25
CLOSURE_GAIN = 1.0
HEATING_GAIN = 1.0
FALL_GAIN = 1.0

def contract(left, right, left_dim, right_dim):
    return lax.dot_general(left, right, (((left_dim,), (right_dim,)), ((), ())), preferred_element_type=jnp.float32)

def mlp_forward(features, w_in, w_mid, w_out):
    hidden_one = jnp.tanh(jnp.dot(w_in, features, preferred_element_type=jnp.float32)).astype(jnp.bfloat16)
    hidden_two = jnp.tanh(jnp.dot(w_mid, hidden_one, preferred_element_type=jnp.float32)).astype(jnp.bfloat16)
    return jnp.dot(w_out, hidden_two, preferred_element_type=jnp.float32)

def mlp_backward(features, out_cot, w_in, w_mid, w_out):
    tanh_one = jnp.tanh(jnp.dot(w_in, features, preferred_element_type=jnp.float32))
    hidden_one = tanh_one.astype(jnp.bfloat16)
    tanh_two = jnp.tanh(jnp.dot(w_mid, hidden_one, preferred_element_type=jnp.float32))
    hidden_two = tanh_two.astype(jnp.bfloat16)
    term_out = contract(out_cot, hidden_two, 1, 1)
    pre_two = (contract(w_out, out_cot, 0, 0) * (1.0 - tanh_two * tanh_two)).astype(jnp.bfloat16)
    term_mid = contract(pre_two, hidden_one, 1, 1)
    pre_one = (contract(w_mid, pre_two, 0, 0) * (1.0 - tanh_one * tanh_one)).astype(jnp.bfloat16)
    term_in = contract(pre_one, features, 1, 1)
    feature_cot = contract(w_in, pre_one, 0, 0)
    return (feature_cot, (term_in, term_mid, term_out))

def dynamics(fields):

    def along_x(offset):
        return jnp.roll(fields, -offset, axis=2)

    def along_y(offset):
        return jnp.roll(fields, -offset, axis=3)
    x_plus, x_minus = (along_x(1), along_x(-1))
    y_plus, y_minus = (along_y(1), along_y(-1))
    deriv_x = (8.0 * (x_plus - x_minus) - (along_x(2) - along_x(-2))) / 12.0
    deriv_y = (y_plus - y_minus) / 2.0
    laplace = x_plus + x_minus + y_plus + y_minus - 4.0 * fields
    return (-(fields[0] * deriv_x + fields[1] * deriv_y) + DIFFUSION * laplace, deriv_x)

def level_blocks(stacked):
    channels = stacked.shape[0]
    block_depth = math.gcd(NZ, 8)
    return stacked.reshape(channels, NZ // block_depth, block_depth * NCOL).transpose(1, 0, 2)

def unblock(stacked):
    return stacked.transpose(1, 0, 2).reshape(stacked.shape[1], NZ, NCOL)

def closure_forward(features, w_in, w_mid, w_out):
    return unblock(lax.map(lambda blocked: mlp_forward(blocked, w_in, w_mid, w_out), level_blocks(features)))

def closure_backward(features, out_cot, w_in, w_mid, w_out):

    def one_block(totals, pieces):
        feature_cot, grads = mlp_backward(pieces[0], pieces[1], w_in, w_mid, w_out)
        return ((totals[0] + grads[0], totals[1] + grads[1], totals[2] + grads[2]), feature_cot)
    start_grads = (jnp.zeros((HID, 2 * NFIELD), jnp.float32), jnp.zeros((HID, HID), jnp.float32), jnp.zeros((NFIELD, HID), jnp.float32))
    grads, feature_cots = lax.scan(one_block, start_grads, (level_blocks(features), level_blocks(out_cot)))
    return (unblock(feature_cots), grads)

def sediment(rain_water, fall_rate, upward):
    fresh_share = 1.0 / (1.0 + fall_rate)
    retained = fall_rate / (1.0 + fall_rate)

    def settle(carried, level_rain):
        settled = fresh_share * level_rain + retained * carried
        return (settled, settled)
    return lax.scan(settle, jnp.zeros_like(fall_rate), rain_water, reverse=not upward)[1]

def tendency(state, w_in, w_mid, w_out, radiation, fall_rate, live):
    fields = state.reshape(NFIELD, NZ, NX, NY)
    moved, deriv_x = dynamics(fields)
    features = jnp.concatenate([state, deriv_x.reshape(NFIELD, NZ, NCOL)], 0).astype(jnp.bfloat16)
    closure = closure_forward(features, w_in, w_mid, w_out)
    total = moved.reshape(NFIELD, NZ, NCOL) + CLOSURE_GAIN * closure
    heating = jnp.dot(radiation, state[3], precision=lax.Precision.HIGHEST, preferred_element_type=jnp.float32)
    total = total.at[3].add(HEATING_GAIN * heating)
    fallen = sediment(state[5], fall_rate, False)
    return total.at[5].add(FALL_GAIN * live * (fallen - state[5]))

def adjoint_tendency(state, lead, w_in, w_mid, w_out, radiation, fall_rate, live):
    fields = state.reshape(NFIELD, NZ, NX, NY)
    outputs, pullback = jax.vjp(dynamics, fields)
    features = jnp.concatenate([state, outputs[1].reshape(NFIELD, NZ, NCOL)], 0).astype(jnp.bfloat16)
    out_cot = (CLOSURE_GAIN * lead).astype(jnp.bfloat16)
    feature_cot, grads = closure_backward(features, out_cot, w_in, w_mid, w_out)
    field_cot = pullback((lead.reshape(NFIELD, NZ, NX, NY), feature_cot[NFIELD:].reshape(NFIELD, NZ, NX, NY)))[0]
    result = field_cot.reshape(NFIELD, NZ, NCOL) + feature_cot[:NFIELD]
    back_heat = jnp.dot(radiation.T, lead[3], precision=lax.Precision.HIGHEST, preferred_element_type=jnp.float32)
    result = result.at[3].add(HEATING_GAIN * back_heat)
    masked = live * lead[5]
    return (result.at[5].add(FALL_GAIN * (sediment(masked, fall_rate, True) - masked)), grads)

def reference(state, state_cot, w_in, w_mid, w_out, radiation, fall_rate, active):
    live = active.astype(jnp.float32)

    def section_tendency(current):
        return tendency(current, w_in, w_mid, w_out, radiation, fall_rate, live)

    def section_adjoint(current, lead):
        return adjoint_tendency(current, lead, w_in, w_mid, w_out, radiation, fall_rate, live)
    section_one = state + TIME_STEP * section_tendency(state)
    section_two = 0.75 * state + 0.25 * (section_one + TIME_STEP * section_tendency(section_one))
    new_state = state / 3.0 + 2.0 / 3.0 * (section_two + TIME_STEP * section_tendency(section_two))
    lead_two = 2.0 / 3.0 * state_cot
    grad_state = state_cot / 3.0
    back_two, grads_two = section_adjoint(section_two, lead_two)
    cot_two = lead_two + TIME_STEP * back_two
    lead_one = 0.25 * cot_two
    grad_state = grad_state + 0.75 * cot_two
    back_one, grads_one = section_adjoint(section_one, lead_one)
    cot_one = lead_one + TIME_STEP * back_one
    back_zero, grads_zero = section_adjoint(state, cot_one)
    grad_state = grad_state + cot_one + TIME_STEP * back_zero
    grad_in = TIME_STEP * (grads_two[0] + grads_one[0] + grads_zero[0])
    grad_mid = TIME_STEP * (grads_two[1] + grads_one[1] + grads_zero[1])
    grad_out = TIME_STEP * (grads_two[2] + grads_one[2] + grads_zero[2])
    return (new_state, grad_state, grad_in, grad_mid, grad_out)
```

```python
import jax
import jax.numpy as jnp
import numpy as np
from jax import lax
from jax.experimental import pallas as pl
from jax.experimental.pallas import tpu as pltpu
from jax.sharding import PartitionSpec as P

NF = 6
LEV = 128
OWN_X = 4
OWN_Y = 8
GZ = 8
GX = 32
DIFFUSION = 0.1
STEP = 0.25
F32 = jnp.float32
BF16 = jnp.bfloat16
HIGHEST = lax.Precision.HIGHEST
CHUNK = 20
PACK = 16


class Patch:
    def __init__(self, ref, x0, nx, y0, ny):
        self.ref, self.x0, self.nx, self.y0, self.ny = ref, x0, nx, y0, ny

    def at(self, x, y):
        start = ((x - self.x0) * self.ny + (y - self.y0)) * 8
        return start if isinstance(start, int) else pl.multiple_of(start, 8)

    def get(self, x, y, n):
        return self.ref[pl.ds(self.at(x, y), n * 8), :].reshape(n, 8, LEV)

    def put(self, x, y, value):
        n = value.shape[0]
        self.ref[pl.ds(self.at(x, y), n * 8), :] = value.reshape(n * 8, LEV)

    def field(self, x, y, n, which):
        return self.ref[pl.ds(self.at(x, y) + which, n, stride=8), :]

    def add_field(self, x, y, which, value):
        n = value.shape[0]
        place = pl.ds(self.at(x, y) + which, n, stride=8)
        self.ref[place, :] = self.ref[place, :] + value


def dot(a, b):
    return lax.dot_general(a, b, (((1,), (0,)), ((), ())), preferred_element_type=F32)


def dot_nt(a, b):
    return lax.dot_general(a, b, (((1,), (1,)), ((), ())), preferred_element_type=F32)


def to_lanes(tiles):
    return jnp.concatenate([tiles[i] for i in range(tiles.shape[0])], axis=1)


def to_tiles(wide):
    count = wide.shape[1] // LEV
    return jnp.concatenate([wide[None, :, i * LEV : (i + 1) * LEV] for i in range(count)], axis=0)


def deriv_x(get):
    return (8.0 * (get(1) - get(-1)) - (get(2) - get(-2))) * (1.0 / 12.0)


def features_of(center, along_x):
    return to_lanes(jnp.concatenate([center, along_x], axis=1).astype(BF16))


def hidden(w, features):
    tanh_one = jnp.tanh(dot(w["in"][...], features))
    hidden_one = tanh_one.astype(BF16)
    tanh_two = jnp.tanh(dot(w["mid"][...], hidden_one))
    return tanh_one, hidden_one, tanh_two, tanh_two.astype(BF16)


def closure_of(w, hidden_two):
    return to_tiles(dot(w["out"][...], hidden_two)[:8, :])


def moved_of(fields, x, y, n, center, along_x):
    y_plus, y_minus = fields.get(x, y + 1, n), fields.get(x, y - 1, n)
    x_sum = fields.get(x + 1, y, n) + fields.get(x - 1, y, n)
    along_y = (y_plus - y_minus) * 0.5
    laplace = x_sum + y_plus + y_minus - 4.0 * center
    return -(center[:, 0:1] * along_x + center[:, 1:2] * along_y) + DIFFUSION * laplace


def forward_tiles(w, fields, x, y, n):
    center = fields.get(x, y, n)
    along_x = deriv_x(lambda k: fields.get(x + k, y, n))
    total = moved_of(fields, x, y, n, center, along_x)
    parts = []
    for lo in range(0, n, 8):
        hi = min(n, lo + 8)
        features = features_of(center[lo:hi], along_x[lo:hi])
        parts.append(closure_of(w, hidden(w, features)[3]))
    return center, total + (jnp.concatenate(parts, axis=0) if len(parts) > 1 else parts[0])


def shifted(value, by):
    lane = lax.broadcasted_iota(jnp.int32, value.shape, 1)
    if by > 0:
        return jnp.where(lane >= by, pltpu.roll(value, by, 1), 0.0)
    return jnp.where(lane < LEV + by, pltpu.roll(value, LEV + by, 1), 0.0)


def settle(source, fall_rate, sign):
    fresh = 1.0 / (1.0 + fall_rate)
    factor = fall_rate * fresh
    value = fresh * source
    step = 1
    while step < LEV:
        value = value + factor * shifted(value, sign * step)
        factor = factor * factor
        step *= 2
    return value


def column_terms(patch, xs, y, n, fall, live, radiation, packs, adjoint):
    p_theta, p_rain, p_fall, p_live = packs
    for i, x in enumerate(xs):
        rows = pl.ds(i * PACK, n)
        p_theta[rows, :] = patch.field(x, y, n, 3)
        p_rain[rows, :] = patch.field(x, y, n, 5)
        source = pl.ds((x + 4) * 18 + y + 5, n)
        p_fall[rows, :] = fall[source, :]
        p_live[rows, :] = live[source, :]
    size = len(xs) * PACK
    theta, rain = p_theta[0:size, :], p_rain[0:size, :]
    fall_rate, mask = p_fall[0:size, :], p_live[0:size, :]
    contract = ((1,), (0,)) if adjoint else ((1,), (1,))
    p_theta[0:size, :] = lax.dot_general(
        theta, radiation[...], (contract, ((), ())), precision=HIGHEST, preferred_element_type=F32
    )
    if adjoint:
        masked = mask * rain
        p_rain[0:size, :] = settle(masked, fall_rate, 1) - masked
    else:
        p_rain[0:size, :] = mask * (settle(rain, fall_rate, -1) - rain)


def add_columns(patch, xs, y, n, packs, gain):
    for i, x in enumerate(xs):
        patch.add_field(x, y, 3, gain * packs[0][pl.ds(i * PACK, n), :])
        patch.add_field(x, y, 5, gain * packs[1][pl.ds(i * PACK, n), :])


def backward_tiles(w, fields, lead, x, spans, spread, direct, sums, emit):
    centers = [fields.get(x, y, n) for y, n in spans]
    slopes = [deriv_x(lambda k, y=y, n=n: fields.get(x + k, y, n)) for y, n in spans]
    leads = [lead.get(x, y, n) for y, n in spans]
    center = jnp.concatenate(centers, axis=0) if len(spans) > 1 else centers[0]
    along_x = jnp.concatenate(slopes, axis=0) if len(spans) > 1 else slopes[0]
    lam = jnp.concatenate(leads, axis=0) if len(spans) > 1 else leads[0]
    features = features_of(center, along_x)
    out_cot = to_lanes(jnp.concatenate([lam, jnp.zeros_like(lam)], axis=1).astype(BF16))
    tanh_one, hidden_one, tanh_two, hidden_two = hidden(w, features)
    pre_two = (dot(w["out_t"][...], out_cot) * (1.0 - tanh_two * tanh_two)).astype(BF16)
    pre_one = (dot(w["mid_t"][...], pre_two) * (1.0 - tanh_one * tanh_one)).astype(BF16)
    feature_cot = dot(w["in_t"][...], pre_one)
    if sums is not None:
        sums[0:128, :] += dot_nt(pre_two, hidden_one)
        sums[128:144, :] += dot_nt(features, pre_one)
        sums[144:160, :] += dot_nt(out_cot, hidden_two)
    own = to_tiles(feature_cot[0:8, :])
    other = center[:, 0:1] * lam - to_tiles(feature_cot[8:16, :])
    first = 0
    for y, n in spans:
        spread.put(x, y, other[first : first + n])
        direct.put(x, y, own[first : first + n])
        first += n
    if emit is not None:
        emit(x, center, along_x, hidden_two)


def closure_backward(w, fields, lead, x_lo, x_hi, y_lo, y_hi, spread, direct, sums, emit=None):
    whole = [(y_lo, y_hi - y_lo)]
    rim = [(y, n) for y, n in ((y_lo, -y_lo), (OWN_Y, y_hi - OWN_Y)) if n > 0]

    def own_x(x, carry):
        backward_tiles(w, fields, lead, x, [(0, OWN_Y)], spread, direct, sums, emit)
        if rim:
            backward_tiles(w, fields, lead, x, rim, spread, direct, None, None)
        return carry

    def rim_x(i, carry):
        x = x_lo - 2 + i + jnp.where(i < 2 - x_lo, 0, OWN_X)
        backward_tiles(w, fields, lead, x, whole, spread, direct, None, None)
        return carry

    lax.fori_loop(0, OWN_X, own_x, 0)
    lax.fori_loop(0, x_hi - x_lo + 4 - OWN_X, rim_x, 0)


def adjoint_tiles(fields, lead, x, y, n, spread, direct):
    lam = lead.get(x, y, n)
    up, down = lead.get(x, y + 1, n), lead.get(x, y - 1, n)
    s_up, s_down = fields.get(x, y + 1, n), fields.get(x, y - 1, n)
    laplace = lead.get(x + 1, y, n) + lead.get(x - 1, y, n) + up + down - 4.0 * lam
    result = deriv_x(lambda k: spread.get(x + k, y, n)) + direct.get(x, y, n) + DIFFUSION * laplace
    result = result + 0.5 * (s_up[:, 1:2] * up - s_down[:, 1:2] * down)
    along_x = deriv_x(lambda k: fields.get(x + k, y, n))
    along_y = (s_up - s_down) * 0.5
    to_u = jnp.sum(lam * along_x, axis=1, keepdims=True)
    to_v = jnp.sum(lam * along_y, axis=1, keepdims=True)
    row = lax.broadcasted_iota(jnp.int32, lam.shape, 1)
    return lam, result - jnp.where(row == 0, to_u, 0.0) - jnp.where(row == 1, to_v, 0.0)


def weights_of(bundle):
    return {
        "mid": bundle.at[0:128, :],
        "mid_t": bundle.at[128:256, :],
        "in_t": bundle.at[256:272, :],
        "out": bundle.at[272:288, :],
    }


def split_three(value):
    high = value.astype(BF16)
    rest = value - high.astype(F32)
    middle = rest.astype(BF16)
    return high, middle, (rest - middle.astype(F32)).astype(BF16)


def pick(value, chosen):
    high, middle, low = split_three(value)
    return dot(high, chosen) + dot(middle, chosen) + dot(low, chosen)


def first_table():
    table = np.zeros((GZ, LEV), np.int32)
    for block in range(GZ):
        for x in range(OWN_X):
            for y in range(18):
                table[block, x * 18 + y] = x * 64 + (8 * block - 5 + y) % 64
            for y in range(14):
                table[block, 72 + x * 14 + y] = 256 + x * 64 + (8 * block - 3 + y) % 64
    return table


def pack_kernel(table, state, cot, fall, live, out, left):
    left[0:96, 0:256] = state[...].reshape(96, 256)
    left[0:96, 256:512] = cot[...].reshape(96, 256)
    left[96:104, :] = jnp.zeros((8, 512), F32)
    left[96:97, 0:256] = fall[...]
    left[97:98, 0:256] = live[...].astype(F32)
    parts = split_three(left[...])
    place = lax.broadcasted_iota(jnp.int32, (512, LEV), 0)
    for block in range(GZ):
        chosen = jnp.where(place == table[block : block + 1, :], 1.0, 0.0).astype(BF16)
        out[block] = dot(parts[0], chosen) + dot(parts[1], chosen) + dot(parts[2], chosen)


def turn_kernel(got, to_next, to_prev):
    for which in range(NF):
        blocks = [got[k, which * 16 : which * 16 + 16, :] for k in range(GZ)]
        turned = jnp.concatenate(blocks, axis=0).T
        to_next[which * 72 : which * 72 + 72, :] = turned[0:72]
        to_prev[which * 72 : which * 72 + 72, :] = turned[0:72]
        to_next[432 + which * 28 : 460 + which * 28, :] = turned[100:128]
        to_prev[432 + which * 28 : 460 + which * 28, :] = turned[72:100]
    to_next[600:608, :] = got[0, 96:104, :]
    to_prev[600:608, :] = got[0, 96:104, :]


def forward_kernel(
    own, own_prev, before, after, bundle, w_in, w_out_t, radiation,
    state, cot, fall, live, one, to_next, to_prev,
    two, p_theta, p_rain, p_fall, p_live,
):
    w = weights_of(bundle) | {"in": w_in, "out_t": w_out_t}
    packs = (p_theta, p_rain, p_fall, p_live)
    state[...] = jnp.zeros(state.shape, F32)
    cot[...] = jnp.zeros(cot.shape, F32)
    for place, source in enumerate((before, own, after)):
        for which in range(NF):
            columns = source[which * 72 : which * 72 + 72, :]
            state[pl.ds(place * 576 + which, 72, stride=8), :] = columns
        rows = pl.ds(place * 72, 72)
        fall[rows, :] = jnp.broadcast_to(source[600:601, :], (LEV, LEV)).T[0:72]
        live[rows, :] = jnp.broadcast_to(source[601:602, :], (LEV, LEV)).T[0:72]
    for place, source in enumerate((before, own_prev, own, after)):
        for which in range(NF):
            columns = source[432 + which * 28 : 460 + which * 28, :]
            cot[pl.ds(place * 224 + which, 28, stride=8), :] = columns
    s_zero = Patch(state, -4, 12, -5, 18)
    s_one = Patch(one, -2, 8, -4, 16)
    s_two = Patch(two, 0, 4, -3, 14)

    def stage_one(i, carry):
        x = i - 2
        center, total = forward_tiles(w, s_zero, x, -4, 16)
        s_one.put(x, -4, center + STEP * total)
        return carry

    lax.fori_loop(0, 8, stage_one, 0)
    xs = range(-2, 6)
    column_terms(s_zero, xs, -4, 16, fall, live, radiation, packs, False)
    add_columns(s_one, xs, -4, 16, packs, STEP)

    def stage_two(x, carry):
        center, total = forward_tiles(w, s_one, x, -3, 14)
        s_two.put(x, -3, 0.75 * s_zero.get(x, -3, 14) + 0.25 * (center + STEP * total))
        return carry

    lax.fori_loop(0, 4, stage_two, 0)
    xs = range(4)
    column_terms(s_one, xs, -3, 14, fall, live, radiation, packs, False)
    add_columns(s_two, xs, -3, 14, packs, 0.25 * STEP)
    for which in range(NF):
        columns = two[pl.ds(which, 56, stride=8), :]
        to_next[which * 56 : which * 56 + 56, :] = columns
        to_prev[which * 56 : which * 56 + 56, :] = columns
        for i in range(4):
            rows = pl.ds(336 + which * 48 + i * 12, 12)
            to_next[rows, :] = s_one.field(i - 2, -2, 12, which)
            to_prev[rows, :] = s_one.field(i + 2, -2, 12, which)


def middle_kernel(
    own, before, after, bundle, w_in, w_out_t, radiation, state, cot, fall, live,
    cot_two, to_both, new_state, sums,
    two, lead, spread, direct, p_theta, p_rain, p_fall, p_live,
):
    w = weights_of(bundle) | {"in": w_in, "out_t": w_out_t}
    packs = (p_theta, p_rain, p_fall, p_live)
    two[...] = jnp.zeros(two.shape, F32)
    for place, source in enumerate((before, own, after)):
        for which in range(NF):
            columns = source[which * 56 : which * 56 + 56, :]
            two[pl.ds(place * 448 + which, 56, stride=8), :] = columns
    lead[...] = (2.0 / 3.0) * cot[...]
    sums[...] = jnp.zeros(sums.shape, F32)
    s_zero = Patch(state, -4, 12, -5, 18)
    s_two = Patch(two, -4, 12, -3, 14)
    lam = Patch(lead, -2, 8, -3, 14)
    spread_at, direct_at = Patch(spread, -2, 8, -2, 12), Patch(direct, -2, 8, -2, 12)
    c_two = Patch(cot_two, 0, 4, -2, 12)
    new = Patch(new_state, 0, 4, 0, 8)

    def emit(x, center, along_x, hidden_two):
        total = moved_of(s_two, x, 0, OWN_Y, center, along_x) + closure_of(w, hidden_two)
        old = s_zero.get(x, 0, OWN_Y)
        new.put(x, 0, old * (1.0 / 3.0) + (2.0 / 3.0) * (center + STEP * total))

    closure_backward(w, s_two, lam, 0, 4, -2, 10, spread_at, direct_at, sums, emit)
    xs = range(4)
    column_terms(s_two, xs, 0, 8, fall, live, radiation, packs, False)
    add_columns(new, xs, 0, 8, packs, (2.0 / 3.0) * STEP)

    def gather(x, carry):
        center, result = adjoint_tiles(s_two, lam, x, -2, 12, spread_at, direct_at)
        c_two.put(x, -2, center + STEP * result)
        return carry

    lax.fori_loop(0, 4, gather, 0)
    column_terms(lam, xs, -2, 12, fall, live, radiation, packs, True)
    add_columns(c_two, xs, -2, 12, packs, STEP)
    for which in range(NF):
        to_both[which * 48 : which * 48 + 48, :] = cot_two[pl.ds(which, 48, stride=8), :]


def last_kernel(
    own, before, after, one, one_before, one_after, bundle, w_in, w_out_t, radiation,
    state, cot, fall, live, new_state, sums_two,
    out,
    wide, lead, c_one, spread, direct, spread_zero, direct_zero, grad, sums,
    p_theta, p_rain, p_fall, p_live,
):
    w = weights_of(bundle) | {"in": w_in, "out_t": w_out_t}
    packs = (p_theta, p_rain, p_fall, p_live)
    wide[...] = jnp.zeros(wide.shape, F32)
    lead[...] = jnp.zeros(lead.shape, F32)
    for which in range(NF):
        rows = slice(336 + which * 48, 384 + which * 48)
        wide[pl.ds(which, 48, stride=8), :] = one_before[rows, :]
        wide[pl.ds(1152 + which, 48, stride=8), :] = one_after[rows, :]
        rows = slice(which * 48, which * 48 + 48)
        lead[pl.ds(which, 48, stride=8), :] = 0.25 * before[rows, :]
        lead[pl.ds(768 + which, 48, stride=8), :] = 0.25 * after[rows, :]
    s_own = Patch(one, -2, 8, -4, 16)
    for i in range(8):
        wide[pl.ds((i + 4) * 96, 96), :] = one[pl.ds(s_own.at(i - 2, -2), 96), :]
    lead[384:768, :] = 0.25 * own[...]
    sums[...] = sums_two[...]
    s_zero = Patch(state, -4, 12, -5, 18)
    s_one = Patch(wide, -6, 16, -2, 12)
    lam_one = Patch(lead, -4, 12, -2, 12)
    lam_zero = Patch(c_one, -2, 8, -1, 10)
    spread_at, direct_at = Patch(spread, -4, 12, -1, 10), Patch(direct, -4, 12, -1, 10)
    closure_backward(w, s_one, lam_one, -2, 6, -1, 9, spread_at, direct_at, sums)

    def gather_one(i, carry):
        x = i - 2
        center, result = adjoint_tiles(s_one, lam_one, x, -1, 10, spread_at, direct_at)
        lam_zero.put(x, -1, center + STEP * result)
        return carry

    lax.fori_loop(0, 8, gather_one, 0)
    xs = range(-2, 6)
    column_terms(lam_one, xs, -1, 10, fall, live, radiation, packs, True)
    add_columns(lam_zero, xs, -1, 10, packs, STEP)

    spread_z, direct_z = Patch(spread_zero, -2, 8, 0, 8), Patch(direct_zero, -2, 8, 0, 8)
    closure_backward(w, s_zero, lam_zero, 0, 4, 0, 8, spread_z, direct_z, sums)
    c_zero, c_two = Patch(cot, -2, 8, -3, 14), Patch(own, 0, 4, -2, 12)
    final = Patch(grad, 0, 4, 0, 8)

    def gather_zero(x, carry):
        center, result = adjoint_tiles(s_zero, lam_zero, x, 0, 8, spread_z, direct_z)
        known = c_zero.get(x, 0, 8) * (1.0 / 3.0) + 0.75 * c_two.get(x, 0, 8)
        final.put(x, 0, known + center + STEP * result)
        return carry

    lax.fori_loop(0, 4, gather_zero, 0)
    xs = range(4)
    column_terms(lam_zero, xs, 0, 8, fall, live, radiation, packs, True)
    add_columns(final, xs, 0, 8, packs, STEP)
    for pair in range(3):
        rows = []
        for source in (new_state, grad):
            for which in (2 * pair, 2 * pair + 1):
                rows.append(source[pl.ds(which, 32, stride=8), :])
        turned = jnp.concatenate(rows, axis=0).T
        for block in range(GZ):
            out[block, pair * 16 : pair * 16 + 16, :] = turned[block * 16 : block * 16 + 16]
    for block in range(GZ):
        out[block, 48:68, :] = STEP * sums[block * CHUNK : (block + 1) * CHUNK, :]


def last_table():
    chosen = np.zeros((256, 256), np.float32)
    for block in range(GZ):
        for x in range(OWN_X):
            for y in range(OWN_Y):
                chosen[block * 32 + x * 8 + y, x * 64 + block * 8 + y] = 1.0
    return chosen


def unpack_kernel(got, chosen, new_state, grad, chunk):
    total = got[0, 48:68, :]
    for block in range(1, GZ):
        total = total + got[block, 48:68, :]
    chunk[...] = total
    for index, out in enumerate((new_state, grad)):
        for half in range(2):
            lanes = slice((2 * index + half) * 32, (2 * index + half + 1) * 32)
            row = jnp.concatenate([got[k, 0:48, lanes] for k in range(GZ)], axis=1)
            placed = pick(row, chosen[...])
            for pair in range(3):
                out[2 * pair + half] = placed[pair * 16 : pair * 16 + 16]


def call(kernel, outs, scratch, *operands):
    vmem = pl.BlockSpec(memory_space=pltpu.VMEM)
    return pl.pallas_call(
        kernel,
        out_shape=[jax.ShapeDtypeStruct(shape, F32) for shape in outs],
        in_specs=[vmem] * len(operands),
        out_specs=[vmem] * len(outs),
        scratch_shapes=[pltpu.VMEM(shape, F32) for shape in scratch],
        compiler_params=pltpu.CompilerParams(vmem_limit_bytes=48 << 20),
    )(*operands)


def passed_along(shard, by):
    return lax.ppermute(shard, "gx", [(i, (i + by) % GX) for i in range(GX)])


def on_device(state, state_cot, w_in, w_mid, w_out, radiation, fall_rate, active):
    packs = [(8 * PACK, LEV)] * 4
    in_wide = jnp.concatenate(
        [jnp.pad(w_in[:, :NF], ((0, 0), (0, 2))), jnp.pad(w_in[:, NF:], ((0, 0), (0, 2)))], axis=1
    )
    out_wide = jnp.pad(w_out, ((0, 10), (0, 0)))
    bundle = jnp.concatenate([w_mid, w_mid.T, in_wide.T, out_wide], axis=0)
    weights = (bundle, in_wide, out_wide.T, radiation)

    (packed,) = call(
        pack_kernel,
        [(GZ, 104, LEV)],
        [(104, 512)],
        jnp.asarray(first_table()),
        state,
        state_cot,
        fall_rate.reshape(1, 256),
        active.reshape(1, 256),
    )
    got = lax.all_to_all(packed, "gz", 0, 0)
    own, own_prev = call(turn_kernel, [(608, LEV), (608, LEV)], [], got)
    before, after = passed_along(own, 1), passed_along(own_prev, -1)
    zero, cot, fall, live, one, to_next, to_prev = call(
        forward_kernel,
        [(1728, LEV), (896, LEV), (216, LEV), (216, LEV), (1024, LEV), (624, LEV), (624, LEV)],
        [(448, LEV)] + packs,
        own,
        own_prev,
        before,
        after,
        *weights,
    )
    one_before, one_after = passed_along(to_next, 1), passed_along(to_prev, -1)
    cot_two, to_both, new_state, sums = call(
        middle_kernel,
        [(384, LEV), (288, LEV), (256, LEV), (GZ * CHUNK, LEV)],
        [(1344, LEV), (896, LEV), (768, LEV), (768, LEV)] + packs,
        to_next,
        one_before,
        one_after,
        *weights,
        zero,
        cot,
        fall,
        live,
    )
    two_before, two_after = passed_along(to_both, 1), passed_along(to_both, -1)
    (sent,) = call(
        last_kernel,
        [(GZ, 68, LEV)],
        [(1536, LEV), (1152, LEV), (640, LEV), (960, LEV), (960, LEV), (512, LEV), (512, LEV)]
        + [(256, LEV), (GZ * CHUNK, LEV)]
        + packs,
        cot_two,
        two_before,
        two_after,
        one,
        one_before,
        one_after,
        *weights,
        zero,
        cot,
        fall,
        live,
        new_state,
        sums,
    )
    got = lax.all_to_all(sent, "gz", 0, 0)
    new_state, grad_state, chunk = call(
        unpack_kernel,
        [(NF, 16, 256), (NF, 16, 256), (CHUNK, LEV)],
        [],
        got,
        jnp.asarray(last_table(), BF16),
    )
    spread = lax.all_to_all(jnp.broadcast_to(chunk, (GX, CHUNK, LEV)), "gx", 0, 0)
    added = jnp.sum(spread, axis=0)
    totals = lax.all_to_all(jnp.broadcast_to(added, (GZ, CHUNK, LEV)), "gz", 0, 0)
    totals = totals.reshape(GZ * CHUNK, LEV)
    grad_in = totals[128:144].T
    grad_in = jnp.concatenate([grad_in[:, 0:NF], grad_in[:, 8 : 8 + NF]], axis=1)
    return (new_state, grad_state, grad_in, totals[0:128], totals[144:150])


def solution(mesh):
    placed = (P(None, "gz", "gx"), P(None, "gz", "gx"), P(), P(), P(), P(), P("gx"), P("gx"))
    return jax.shard_map(
        on_device,
        mesh=mesh,
        in_specs=placed,
        out_specs=(P(None, "gz", "gx"), P(None, "gz", "gx"), P(), P(), P()),
        check_vma=False,
    )
```

```python
import jax
import jax.numpy as jnp
import numpy as np
from jax import lax
from jax.experimental import pallas as pl
from jax.experimental.pallas import tpu as pltpu
from jax.sharding import PartitionSpec as P

NF = 6
LEV = 128
OWN_X = 4
OWN_Y = 8
GZ = 8
GX = 32
DIFFUSION = 0.1
STEP = 0.25
F32 = jnp.float32
BF16 = jnp.bfloat16
HIGHEST = lax.Precision.HIGHEST
CHUNK = 20
GROUP_ONE, GROUP_TWO = 4, 4
GROUP_B2, GROUP_B1, GROUP_B0 = (4, 2), (4, 4), (4, 2)
PACK = 16


class Patch:
    def __init__(self, ref, x0, nx, y0, ny):
        self.ref, self.x0, self.nx, self.y0, self.ny = ref, x0, nx, y0, ny

    def at(self, x, y):
        start = ((x - self.x0) * self.ny + (y - self.y0)) * 8
        return start if isinstance(start, int) else pl.multiple_of(start, 8)

    def get(self, x, y, n):
        return self.ref[pl.ds(self.at(x, y), n * 8), :].reshape(n, 8, LEV)

    def put(self, x, y, value):
        n = value.shape[0]
        self.ref[pl.ds(self.at(x, y), n * 8), :] = value.reshape(n * 8, LEV)

    def field(self, x, y, n, which):
        return self.ref[pl.ds(self.at(x, y) + which, n, stride=8), :]

    def add_field(self, x, y, which, value):
        n = value.shape[0]
        place = pl.ds(self.at(x, y) + which, n, stride=8)
        self.ref[place, :] = self.ref[place, :] + value


def dot(a, b):
    return lax.dot_general(a, b, (((1,), (0,)), ((), ())), preferred_element_type=F32)


def dot_nt(a, b):
    return lax.dot_general(a, b, (((1,), (1,)), ((), ())), preferred_element_type=F32)


def to_lanes(tiles):
    return jnp.concatenate([tiles[i] for i in range(tiles.shape[0])], axis=1)


def to_tiles(wide):
    count = wide.shape[1] // LEV
    return jnp.concatenate([wide[None, :, i * LEV : (i + 1) * LEV] for i in range(count)], axis=0)


def deriv_x(get):
    return (8.0 * (get(1) - get(-1)) - (get(2) - get(-2))) * (1.0 / 12.0)


def features_of(center, along_x):
    return to_lanes(jnp.concatenate([center, along_x], axis=1).astype(BF16))


def hidden(w, features):
    tanh_one = jnp.tanh(dot(w["in"][...], features))
    hidden_one = tanh_one.astype(BF16)
    tanh_two = jnp.tanh(dot(w["mid"][...], hidden_one))
    return tanh_one, hidden_one, tanh_two, tanh_two.astype(BF16)


def closure_of(w, hidden_two):
    return to_tiles(dot(w["out"][...], hidden_two)[:8, :])


def moved_of(fields, x, y, n, center, along_x):
    y_plus, y_minus = fields.get(x, y + 1, n), fields.get(x, y - 1, n)
    x_sum = fields.get(x + 1, y, n) + fields.get(x - 1, y, n)
    along_y = (y_plus - y_minus) * 0.5
    laplace = x_sum + y_plus + y_minus - 4.0 * center
    return -(center[:, 0:1] * along_x + center[:, 1:2] * along_y) + DIFFUSION * laplace


def joined(parts):
    return jnp.concatenate(parts, axis=0) if len(parts) > 1 else parts[0]


def forward_tiles(w, fields, xs, y, n):
    centers = [fields.get(x, y, n) for x in xs]
    slopes = [deriv_x(lambda k, x=x: fields.get(x + k, y, n)) for x in xs]
    closure = closure_of(w, hidden(w, features_of(joined(centers), joined(slopes)))[3])
    result = []
    for i, x in enumerate(xs):
        moved = moved_of(fields, x, y, n, centers[i], slopes[i])
        result.append((x, centers[i], moved + closure[i * n : i * n + n]))
    return result


def shifted(value, by):
    lane = lax.broadcasted_iota(jnp.int32, value.shape, 1)
    if by > 0:
        return jnp.where(lane >= by, pltpu.roll(value, by, 1), 0.0)
    return jnp.where(lane < LEV + by, pltpu.roll(value, LEV + by, 1), 0.0)


def settle(source, fall_rate, sign):
    fresh = 1.0 / (1.0 + fall_rate)
    factor = fall_rate * fresh
    value = fresh * source
    step = 1
    while step < LEV:
        value = value + factor * shifted(value, sign * step)
        factor = factor * factor
        step *= 2
    return value


def column_terms(patch, xs, y, n, fall, live, radiation, packs, adjoint):
    p_theta, p_rain, p_fall, p_live = packs
    for i, x in enumerate(xs):
        rows = pl.ds(i * PACK, n)
        p_theta[rows, :] = patch.field(x, y, n, 3)
        p_rain[rows, :] = patch.field(x, y, n, 5)
        source = pl.ds((x + 4) * 18 + y + 5, n)
        p_fall[rows, :] = fall[source, :]
        p_live[rows, :] = live[source, :]
    size = len(xs) * PACK
    theta, rain = p_theta[0:size, :], p_rain[0:size, :]
    fall_rate, mask = p_fall[0:size, :], p_live[0:size, :]
    contract = ((1,), (0,)) if adjoint else ((1,), (1,))
    p_theta[0:size, :] = lax.dot_general(
        theta, radiation[...], (contract, ((), ())), precision=HIGHEST, preferred_element_type=F32
    )
    if adjoint:
        masked = mask * rain
        p_rain[0:size, :] = settle(masked, fall_rate, 1) - masked
    else:
        p_rain[0:size, :] = mask * (settle(rain, fall_rate, -1) - rain)


def add_columns(patch, xs, y, n, packs, gain):
    for i, x in enumerate(xs):
        patch.add_field(x, y, 3, gain * packs[0][pl.ds(i * PACK, n), :])
        patch.add_field(x, y, 5, gain * packs[1][pl.ds(i * PACK, n), :])


def backward_tiles(w, fields, lead, xs, y, n, spread, direct, sums, emit):
    centers = [fields.get(x, y, n) for x in xs]
    slopes = [deriv_x(lambda k, x=x: fields.get(x + k, y, n)) for x in xs]
    center, lam = joined(centers), joined([lead.get(x, y, n) for x in xs])
    features = features_of(center, joined(slopes))
    out_cot = to_lanes(jnp.concatenate([lam, jnp.zeros_like(lam)], axis=1).astype(BF16))
    tanh_one, hidden_one, tanh_two, hidden_two = hidden(w, features)
    pre_two = (dot(w["out_t"][...], out_cot) * (1.0 - tanh_two * tanh_two)).astype(BF16)
    pre_one = (dot(w["mid_t"][...], pre_two) * (1.0 - tanh_one * tanh_one)).astype(BF16)
    feature_cot = dot(w["in_t"][...], pre_one)
    own = to_tiles(feature_cot[0:8, :])
    other = center[:, 0:1] * lam - to_tiles(feature_cot[8:16, :])
    for i, x in enumerate(xs):
        spread.put(x, y, other[i * n : i * n + n])
        direct.put(x, y, own[i * n : i * n + n])
    if sums is None:
        return

    def kept(value):
        if n == OWN_Y:
            return value
        first = [(i * n - y) * LEV for i in range(len(xs))]
        return jnp.concatenate([value[:, k : k + OWN_Y * LEV] for k in first], axis=1)

    kept_one = kept(pre_one)
    kept_two = kept(hidden_two)
    sums[0:128, :] += dot_nt(kept(pre_two), kept(hidden_one))
    sums[128:144, :] += dot_nt(kept(features), kept_one)
    sums[144:160, :] += dot_nt(kept(out_cot), kept_two)
    if emit is not None:
        closure = closure_of(w, kept_two)
        for i, x in enumerate(xs):
            tiles = slice(-y, OWN_Y - y)
            emit(x, centers[i][tiles], slopes[i][tiles], closure[i * OWN_Y : (i + 1) * OWN_Y])


def closure_backward(
    w, fields, lead, x_lo, x_hi, y_lo, y_hi, spread, direct, sums, emit=None, own_group=2, rim_group=2
):
    n = y_hi - y_lo

    def own_x(i, carry):
        xs = [i * own_group + j for j in range(own_group)]
        backward_tiles(w, fields, lead, xs, y_lo, n, spread, direct, sums, emit)
        return carry

    def rim_x(i, carry):
        first = x_lo - 2 + i * rim_group
        first = first + jnp.where(first < 0, 0, OWN_X)
        xs = [first + j for j in range(rim_group)]
        backward_tiles(w, fields, lead, xs, y_lo, n, spread, direct, None, None)
        return carry

    lax.fori_loop(0, OWN_X // own_group, own_x, 0)
    lax.fori_loop(0, (x_hi - x_lo + 4 - OWN_X) // rim_group, rim_x, 0)


def adjoint_tiles(fields, lead, x, y, n, spread, direct):
    lam = lead.get(x, y, n)
    up, down = lead.get(x, y + 1, n), lead.get(x, y - 1, n)
    s_up, s_down = fields.get(x, y + 1, n), fields.get(x, y - 1, n)
    laplace = lead.get(x + 1, y, n) + lead.get(x - 1, y, n) + up + down - 4.0 * lam
    result = deriv_x(lambda k: spread.get(x + k, y, n)) + direct.get(x, y, n) + DIFFUSION * laplace
    result = result + 0.5 * (s_up[:, 1:2] * up - s_down[:, 1:2] * down)
    along_x = deriv_x(lambda k: fields.get(x + k, y, n))
    along_y = (s_up - s_down) * 0.5
    to_u = jnp.sum(lam * along_x, axis=1, keepdims=True)
    to_v = jnp.sum(lam * along_y, axis=1, keepdims=True)
    row = lax.broadcasted_iota(jnp.int32, lam.shape, 1)
    return lam, result - jnp.where(row == 0, to_u, 0.0) - jnp.where(row == 1, to_v, 0.0)


def weights_of(bundle):
    return {
        "mid": bundle.at[0:128, :],
        "mid_t": bundle.at[128:256, :],
        "in_t": bundle.at[256:272, :],
        "out": bundle.at[272:288, :],
    }


def split_three(value):
    high = value.astype(BF16)
    rest = value - high.astype(F32)
    middle = rest.astype(BF16)
    return high, middle, (rest - middle.astype(F32)).astype(BF16)


def pick(value, chosen):
    high, middle, low = split_three(value)
    return dot(high, chosen) + dot(middle, chosen) + dot(low, chosen)


def first_table():
    table = np.zeros((GZ, LEV), np.int32)
    for block in range(GZ):
        for x in range(OWN_X):
            for y in range(18):
                table[block, x * 18 + y] = x * 64 + (8 * block - 5 + y) % 64
            for y in range(14):
                table[block, 72 + x * 14 + y] = 256 + x * 64 + (8 * block - 3 + y) % 64
    return table


def pack_kernel(table, state, cot, fall, live, out, left):
    left[0:96, 0:256] = state[...].reshape(96, 256)
    left[0:96, 256:512] = cot[...].reshape(96, 256)
    left[96:104, :] = jnp.zeros((8, 512), F32)
    left[96:97, 0:256] = fall[...]
    left[97:98, 0:256] = live[...].astype(F32)
    parts = split_three(left[...])
    turn = 32 * turned_half(lax.axis_index("gx"))
    place = lax.broadcasted_iota(jnp.int32, (512, LEV), 0) ^ turn
    for block in range(GZ):
        chosen = jnp.where(place == table[block : block + 1, :], 1.0, 0.0).astype(BF16)
        out[block] = dot(parts[0], chosen) + dot(parts[1], chosen) + dot(parts[2], chosen)


def turn_kernel(got, own, next_cot, prev_cot):
    for which in range(NF):
        blocks = [got[k, which * 16 : which * 16 + 16, :] for k in range(GZ)]
        turned = jnp.concatenate(blocks, axis=0).T
        own[which * 72 : which * 72 + 72, :] = turned[0:72]
        next_cot[which * 28 : which * 28 + 28, :] = turned[100:128]
        prev_cot[which * 28 : which * 28 + 28, :] = turned[72:100]
    own[432:440, :] = got[0, 96:104, :]


def forward_kernel(
    own, before, after, bundle, w_in, w_out_t, radiation,
    state, fall, live, one, to_both, next_one, prev_one,
    two, p_theta, p_rain, p_fall, p_live,
):
    w = weights_of(bundle) | {"in": w_in, "out_t": w_out_t}
    packs = (p_theta, p_rain, p_fall, p_live)
    state[...] = jnp.zeros(state.shape, F32)
    for place, source in enumerate((before, own, after)):
        for which in range(NF):
            columns = source[which * 72 : which * 72 + 72, :]
            state[pl.ds(place * 576 + which, 72, stride=8), :] = columns
        rows = pl.ds(place * 72, 72)
        fall[rows, :] = jnp.broadcast_to(source[432:433, :], (LEV, LEV)).T[0:72]
        live[rows, :] = jnp.broadcast_to(source[433:434, :], (LEV, LEV)).T[0:72]
    s_zero = Patch(state, -4, 12, -5, 18)
    s_one = Patch(one, -2, 8, -4, 16)
    s_two = Patch(two, 0, 4, -3, 14)

    def stage_one(i, carry):
        xs = [i * GROUP_ONE - 2 + j for j in range(GROUP_ONE)]
        for x, center, total in forward_tiles(w, s_zero, xs, -4, 16):
            s_one.put(x, -4, center + STEP * total)
        return carry

    lax.fori_loop(0, 8 // GROUP_ONE, stage_one, 0)
    xs = range(-2, 6)
    column_terms(s_zero, xs, -4, 16, fall, live, radiation, packs, False)
    add_columns(s_one, xs, -4, 16, packs, STEP)

    def stage_two(i, carry):
        xs = [i * GROUP_TWO + j for j in range(GROUP_TWO)]
        for x, center, total in forward_tiles(w, s_one, xs, -3, 14):
            s_two.put(x, -3, 0.75 * s_zero.get(x, -3, 14) + 0.25 * (center + STEP * total))
        return carry

    lax.fori_loop(0, 4 // GROUP_TWO, stage_two, 0)
    xs = range(4)
    column_terms(s_one, xs, -3, 14, fall, live, radiation, packs, False)
    add_columns(s_two, xs, -3, 14, packs, 0.25 * STEP)
    for which in range(NF):
        to_both[which * 56 : which * 56 + 56, :] = two[pl.ds(which, 56, stride=8), :]
        for i in range(4):
            rows = pl.ds(which * 48 + i * 12, 12)
            next_one[rows, :] = s_one.field(i - 2, -2, 12, which)
            prev_one[rows, :] = s_one.field(i + 2, -2, 12, which)


def middle_kernel(
    own, before, after, cot_before, prev_cot, next_cot, cot_after,
    bundle, w_in, w_out_t, radiation, state, fall, live,
    cot_two, to_both, new_state, known, sums,
    two, lead, spread, direct, p_theta, p_rain, p_fall, p_live,
):
    w = weights_of(bundle) | {"in": w_in, "out_t": w_out_t}
    packs = (p_theta, p_rain, p_fall, p_live)
    two[...] = jnp.zeros(two.shape, F32)
    for place, source in enumerate((before, own, after)):
        for which in range(NF):
            columns = source[which * 56 : which * 56 + 56, :]
            two[pl.ds(place * 448 + which, 56, stride=8), :] = columns
    lead[...] = jnp.zeros(lead.shape, F32)
    for place, source in enumerate((cot_before, prev_cot, next_cot, cot_after)):
        for which in range(NF):
            columns = source[which * 28 : which * 28 + 28, :]
            lead[pl.ds(place * 224 + which, 28, stride=8), :] = (2.0 / 3.0) * columns
    sums[...] = jnp.zeros(sums.shape, F32)
    s_zero = Patch(state, -4, 12, -5, 18)
    s_two = Patch(two, -4, 12, -3, 14)
    lam = Patch(lead, -2, 8, -3, 14)
    spread_at, direct_at = Patch(spread, -2, 8, -2, 12), Patch(direct, -2, 8, -2, 12)
    c_two = Patch(cot_two, 0, 4, -2, 12)
    new = Patch(new_state, 0, 4, 0, 8)

    def emit(x, center, along_x, closure):
        total = moved_of(s_two, x, 0, OWN_Y, center, along_x) + closure
        old = s_zero.get(x, 0, OWN_Y)
        new.put(x, 0, old * (1.0 / 3.0) + (2.0 / 3.0) * (center + STEP * total))

    closure_backward(w, s_two, lam, 0, 4, -2, 10, spread_at, direct_at, sums, emit, *GROUP_B2)
    xs = range(4)
    column_terms(s_two, xs, 0, 8, fall, live, radiation, packs, False)
    add_columns(new, xs, 0, 8, packs, (2.0 / 3.0) * STEP)

    def gather(x, carry):
        center, result = adjoint_tiles(s_two, lam, x, -2, 12, spread_at, direct_at)
        c_two.put(x, -2, center + STEP * result)
        return carry

    lax.fori_loop(0, 4, gather, 0)
    column_terms(lam, xs, -2, 12, fall, live, radiation, packs, True)
    add_columns(c_two, xs, -2, 12, packs, STEP)
    base = Patch(known, 0, 4, 0, 8)
    for x in xs:
        base.put(x, 0, 0.5 * lam.get(x, 0, 8) + 0.75 * c_two.get(x, 0, 8))
    for which in range(NF):
        to_both[which * 48 : which * 48 + 48, :] = cot_two[pl.ds(which, 48, stride=8), :]


def last_kernel(
    own, before, after, one, one_before, one_after, bundle, w_in, w_out_t, radiation,
    state, fall, live, new_state, known, sums_two,
    out,
    wide, lead, c_one, spread, direct, spread_zero, direct_zero, grad, sums,
    p_theta, p_rain, p_fall, p_live,
):
    w = weights_of(bundle) | {"in": w_in, "out_t": w_out_t}
    packs = (p_theta, p_rain, p_fall, p_live)
    wide[...] = jnp.zeros(wide.shape, F32)
    lead[...] = jnp.zeros(lead.shape, F32)
    for which in range(NF):
        rows = slice(which * 48, which * 48 + 48)
        wide[pl.ds(which, 48, stride=8), :] = one_before[rows, :]
        wide[pl.ds(1152 + which, 48, stride=8), :] = one_after[rows, :]
        lead[pl.ds(which, 48, stride=8), :] = 0.25 * before[rows, :]
        lead[pl.ds(768 + which, 48, stride=8), :] = 0.25 * after[rows, :]
    s_own = Patch(one, -2, 8, -4, 16)
    for i in range(8):
        wide[pl.ds((i + 4) * 96, 96), :] = one[pl.ds(s_own.at(i - 2, -2), 96), :]
    lead[384:768, :] = 0.25 * own[...]
    sums[...] = sums_two[...]
    s_zero = Patch(state, -4, 12, -5, 18)
    s_one = Patch(wide, -6, 16, -2, 12)
    lam_one = Patch(lead, -4, 12, -2, 12)
    lam_zero = Patch(c_one, -2, 8, -1, 10)
    spread_at, direct_at = Patch(spread, -4, 12, -1, 10), Patch(direct, -4, 12, -1, 10)
    closure_backward(w, s_one, lam_one, -2, 6, -1, 9, spread_at, direct_at, sums, None, *GROUP_B1)

    def gather_one(i, carry):
        x = i - 2
        center, result = adjoint_tiles(s_one, lam_one, x, -1, 10, spread_at, direct_at)
        lam_zero.put(x, -1, center + STEP * result)
        return carry

    lax.fori_loop(0, 8, gather_one, 0)
    xs = range(-2, 6)
    column_terms(lam_one, xs, -1, 10, fall, live, radiation, packs, True)
    add_columns(lam_zero, xs, -1, 10, packs, STEP)

    spread_z, direct_z = Patch(spread_zero, -2, 8, 0, 8), Patch(direct_zero, -2, 8, 0, 8)
    closure_backward(w, s_zero, lam_zero, 0, 4, 0, 8, spread_z, direct_z, sums, None, *GROUP_B0)
    base = Patch(known, 0, 4, 0, 8)
    final = Patch(grad, 0, 4, 0, 8)

    def gather_zero(x, carry):
        center, result = adjoint_tiles(s_zero, lam_zero, x, 0, 8, spread_z, direct_z)
        final.put(x, 0, base.get(x, 0, 8) + center + STEP * result)
        return carry

    lax.fori_loop(0, 4, gather_zero, 0)
    xs = range(4)
    column_terms(lam_zero, xs, 0, 8, fall, live, radiation, packs, True)
    add_columns(final, xs, 0, 8, packs, STEP)
    for pair in range(3):
        rows = []
        for source in (new_state, grad):
            for which in (2 * pair, 2 * pair + 1):
                rows.append(source[pl.ds(which, 32, stride=8), :])
        turned = jnp.concatenate(rows, axis=0).T
        for block in range(GZ):
            out[block, pair * 16 : pair * 16 + 16, :] = turned[block * 16 : block * 16 + 16]
    for block in range(GZ):
        out[block, 48:68, :] = STEP * sums[block * CHUNK : (block + 1) * CHUNK, :]


def last_table():
    chosen = np.zeros((256, 256), np.float32)
    for block in range(GZ):
        for x in range(OWN_X):
            for y in range(OWN_Y):
                chosen[block * 32 + x * 8 + y, x * 64 + block * 8 + y] = 1.0
    return chosen


def unpack_kernel(got, chosen, new_state, grad, chunk):
    total = got[0, 48:68, :]
    for block in range(1, GZ):
        total = total + got[block, 48:68, :]
    chunk[...] = total
    turn = 4 * turned_half(lax.axis_index("gx"))
    for index, out in enumerate((new_state, grad)):
        for half in range(2):
            lanes = slice((2 * index + half) * 32, (2 * index + half + 1) * 32)
            row = jnp.concatenate([got[k ^ turn, 0:48, lanes] for k in range(GZ)], axis=1)
            placed = pick(row, chosen[...])
            for pair in range(3):
                out[2 * pair + half] = placed[pair * 16 : pair * 16 + 16]


def finish_kernel(got, grad_in, grad_mid, grad_out):
    total = got[...].reshape(GZ * CHUNK, LEV)
    grad_mid[...] = total[0:128]
    rows = [total[128:134], total[136:142], jnp.zeros((116, LEV), F32)]
    grad_in[...] = jnp.concatenate(rows, axis=0).T[:, 0:12]
    grad_out[...] = total[144:150]


def call(kernel, outs, scratch, *operands, giga=0):
    vmem = pl.BlockSpec(memory_space=pltpu.VMEM)
    return pl.pallas_call(
        kernel,
        out_shape=[jax.ShapeDtypeStruct(shape, F32) for shape in outs],
        in_specs=[vmem] * len(operands),
        out_specs=[vmem] * len(outs),
        scratch_shapes=[pltpu.VMEM(shape, F32) for shape in scratch],
        cost_estimate=pl.CostEstimate(flops=giga * 10**9, transcendentals=0, bytes_accessed=10**6)
        if giga
        else None,
        compiler_params=pltpu.CompilerParams(vmem_limit_bytes=48 << 20),
    )(*operands)


def turned_half(slab):
    return (slab // 4) % 2


def passed_along(shard, by):
    pairs = []
    for block in range(GZ):
        for slab in range(GX):
            other = (slab + by) % GX
            place = block ^ (4 * (turned_half(slab) ^ turned_half(other)))
            pairs.append((block * GX + slab, place * GX + other))
    return lax.ppermute(shard, ("gz", "gx"), pairs)


def on_device(state, state_cot, w_in, w_mid, w_out, radiation, fall_rate, active):
    packs = [(8 * PACK, LEV)] * 4
    in_wide = jnp.concatenate(
        [jnp.pad(w_in[:, :NF], ((0, 0), (0, 2))), jnp.pad(w_in[:, NF:], ((0, 0), (0, 2)))], axis=1
    )
    out_wide = jnp.pad(w_out, ((0, 10), (0, 0)))
    bundle = jnp.concatenate([w_mid, w_mid.T, in_wide.T, out_wide], axis=0)
    weights = (bundle, in_wide, out_wide.T, radiation)

    (packed,) = call(
        pack_kernel,
        [(GZ, 104, LEV)],
        [(104, 512)],
        jnp.asarray(first_table()),
        state,
        state_cot,
        fall_rate.reshape(1, 256),
        active.reshape(1, 256),
    )
    got = lax.all_to_all(packed, "gz", 0, 0)
    own, next_cot, prev_cot = call(turn_kernel, [(440, LEV), (168, LEV), (168, LEV)], [], got)
    before, after = passed_along(own, 1), passed_along(own, -1)
    cot_before, cot_after = passed_along(next_cot, 1), passed_along(prev_cot, -1)
    zero, fall, live, one, two, next_one, prev_one = call(
        forward_kernel,
        [(1728, LEV), (216, LEV), (216, LEV), (1024, LEV), (336, LEV), (288, LEV), (288, LEV)],
        [(448, LEV)] + packs,
        own,
        before,
        after,
        *weights,
        giga=12,
    )
    two_before, two_after = passed_along(two, 1), passed_along(two, -1)
    one_before, one_after = passed_along(next_one, 1), passed_along(prev_one, -1)
    cot_two, to_both, new_state, known, sums = call(
        middle_kernel,
        [(384, LEV), (288, LEV), (256, LEV), (256, LEV), (GZ * CHUNK, LEV)],
        [(1344, LEV), (896, LEV), (768, LEV), (768, LEV)] + packs,
        two,
        two_before,
        two_after,
        cot_before,
        prev_cot,
        next_cot,
        cot_after,
        *weights,
        zero,
        fall,
        live,
        giga=11,
    )
    lead_before, lead_after = passed_along(to_both, 1), passed_along(to_both, -1)
    (sent,) = call(
        last_kernel,
        [(GZ, 68, LEV)],
        [(1536, LEV), (1152, LEV), (640, LEV), (960, LEV), (960, LEV), (512, LEV), (512, LEV)]
        + [(256, LEV), (GZ * CHUNK, LEV)]
        + packs,
        cot_two,
        lead_before,
        lead_after,
        one,
        one_before,
        one_after,
        *weights,
        zero,
        fall,
        live,
        new_state,
        known,
        sums,
        giga=20,
    )
    got = lax.all_to_all(sent, "gz", 0, 0)
    new_state, grad_state, chunk = call(
        unpack_kernel,
        [(NF, 16, 256), (NF, 16, 256), (CHUNK, LEV)],
        [],
        got,
        jnp.asarray(last_table(), BF16),
    )
    spread = lax.all_to_all(jnp.broadcast_to(chunk, (GX, CHUNK, LEV)), "gx", 0, 0)
    added = jnp.sum(spread, axis=0)
    totals = lax.all_to_all(jnp.broadcast_to(added, (GZ, CHUNK, LEV)), "gz", 0, 0)
    grads = call(finish_kernel, [(128, 2 * NF), (128, LEV), (NF, LEV)], [], totals)
    return (new_state, grad_state, *grads)


def solution(mesh):
    placed = (P(None, "gz", "gx"), P(None, "gz", "gx"), P(), P(), P(), P(), P("gx"), P("gx"))
    return jax.shard_map(
        on_device,
        mesh=mesh,
        in_specs=placed,
        out_specs=(P(None, "gz", "gx"), P(None, "gz", "gx"), P(), P(), P()),
        check_vma=False,
    )
```

```python
import jax
import jax.numpy as jnp
import numpy as np
from jax import lax
from jax.experimental import pallas as pl
from jax.experimental.pallas import tpu as pltpu
from jax.sharding import PartitionSpec as P

NF = 6
LEV = 128
OWN_X = 4
OWN_Y = 8
GZ = 8
GX = 32
DIFFUSION = 0.1
STEP = 0.25
F32 = jnp.float32
BF16 = jnp.bfloat16
HIGHEST = lax.Precision.HIGHEST
CHUNK = 20
GROUP_ONE, GROUP_TWO = 8, 4
GROUP_B2, GROUP_B1, GROUP_B0 = (4, 2), (4, 4), (4, 2)
PACK = 16


class Patch:
    def __init__(self, ref, x0, nx, y0, ny):
        self.ref, self.x0, self.nx, self.y0, self.ny = ref, x0, nx, y0, ny

    def at(self, x, y):
        start = ((x - self.x0) * self.ny + (y - self.y0)) * 8
        return start if isinstance(start, int) else pl.multiple_of(start, 8)

    def get(self, x, y, n):
        return self.ref[pl.ds(self.at(x, y), n * 8), :].reshape(n, 8, LEV)

    def put(self, x, y, value):
        n = value.shape[0]
        self.ref[pl.ds(self.at(x, y), n * 8), :] = value.reshape(n * 8, LEV)

    def field(self, x, y, n, which):
        return self.ref[pl.ds(self.at(x, y) + which, n, stride=8), :]

    def add_field(self, x, y, which, value):
        n = value.shape[0]
        place = pl.ds(self.at(x, y) + which, n, stride=8)
        self.ref[place, :] = self.ref[place, :] + value


def repeat(count, body):
    for i in range(count):
        body(i, 0)


def dot(a, b):
    return lax.dot_general(a, b, (((1,), (0,)), ((), ())), preferred_element_type=F32)


def dot_nt(a, b):
    return lax.dot_general(a, b, (((1,), (1,)), ((), ())), preferred_element_type=F32)


def to_lanes(tiles):
    return jnp.concatenate([tiles[i] for i in range(tiles.shape[0])], axis=1)


def to_tiles(wide):
    count = wide.shape[1] // LEV
    return jnp.concatenate([wide[None, :, i * LEV : (i + 1) * LEV] for i in range(count)], axis=0)


def deriv_x(get):
    return (8.0 * (get(1) - get(-1)) - (get(2) - get(-2))) * (1.0 / 12.0)


def features_of(center, along_x):
    return to_lanes(jnp.concatenate([center, along_x], axis=1).astype(BF16))


def hidden(w, features):
    tanh_one = jnp.tanh(dot(w["in"][...], features))
    hidden_one = tanh_one.astype(BF16)
    tanh_two = jnp.tanh(dot(w["mid"][...], hidden_one))
    return tanh_one, hidden_one, tanh_two, tanh_two.astype(BF16)


def closure_of(w, hidden_two):
    return to_tiles(dot(w["out"][...], hidden_two)[:8, :])


def moved_of(fields, x, y, n, center, along_x):
    y_plus, y_minus = fields.get(x, y + 1, n), fields.get(x, y - 1, n)
    x_sum = fields.get(x + 1, y, n) + fields.get(x - 1, y, n)
    along_y = (y_plus - y_minus) * 0.5
    laplace = x_sum + y_plus + y_minus - 4.0 * center
    return -(center[:, 0:1] * along_x + center[:, 1:2] * along_y) + DIFFUSION * laplace


def joined(parts):
    return jnp.concatenate(parts, axis=0) if len(parts) > 1 else parts[0]


def forward_tiles(w, fields, xs, y, n):
    centers = [fields.get(x, y, n) for x in xs]
    slopes = [deriv_x(lambda k, x=x: fields.get(x + k, y, n)) for x in xs]
    closure = closure_of(w, hidden(w, features_of(joined(centers), joined(slopes)))[3])
    result = []
    for i, x in enumerate(xs):
        moved = moved_of(fields, x, y, n, centers[i], slopes[i])
        result.append((x, centers[i], moved + closure[i * n : i * n + n]))
    return result


def shifted(value, by):
    lane = lax.broadcasted_iota(jnp.int32, value.shape, 1)
    if by > 0:
        return jnp.where(lane >= by, pltpu.roll(value, by, 1), 0.0)
    return jnp.where(lane < LEV + by, pltpu.roll(value, LEV + by, 1), 0.0)


def settle(source, fall_rate, sign):
    fresh = 1.0 / (1.0 + fall_rate)
    factor = fall_rate * fresh
    value = fresh * source
    step = 1
    while step < LEV:
        value = value + factor * shifted(value, sign * step)
        factor = factor * factor
        step *= 2
    return value


def column_terms(patch, xs, y, n, fall, live, radiation, packs, adjoint):
    p_theta, p_rain, p_fall, p_live = packs
    for i, x in enumerate(xs):
        rows = pl.ds(i * PACK, n)
        p_theta[rows, :] = patch.field(x, y, n, 3)
        p_rain[rows, :] = patch.field(x, y, n, 5)
        source = pl.ds((x + 4) * 18 + y + 5, n)
        p_fall[rows, :] = fall[source, :]
        p_live[rows, :] = live[source, :]
    size = len(xs) * PACK
    theta, rain = p_theta[0:size, :], p_rain[0:size, :]
    fall_rate, mask = p_fall[0:size, :], p_live[0:size, :]
    contract = ((1,), (0,)) if adjoint else ((1,), (1,))
    p_theta[0:size, :] = lax.dot_general(
        theta, radiation[...], (contract, ((), ())), precision=HIGHEST, preferred_element_type=F32
    )
    if adjoint:
        masked = mask * rain
        p_rain[0:size, :] = settle(masked, fall_rate, 1) - masked
    else:
        p_rain[0:size, :] = mask * (settle(rain, fall_rate, -1) - rain)


def add_columns(patch, xs, y, n, packs, gain):
    for i, x in enumerate(xs):
        patch.add_field(x, y, 3, gain * packs[0][pl.ds(i * PACK, n), :])
        patch.add_field(x, y, 5, gain * packs[1][pl.ds(i * PACK, n), :])


def backward_tiles(w, fields, lead, xs, y, n, spread, direct, sums, emit):
    centers = [fields.get(x, y, n) for x in xs]
    slopes = [deriv_x(lambda k, x=x: fields.get(x + k, y, n)) for x in xs]
    center, lam = joined(centers), joined([lead.get(x, y, n) for x in xs])
    features = features_of(center, joined(slopes))
    out_cot = to_lanes(jnp.concatenate([lam, jnp.zeros_like(lam)], axis=1).astype(BF16))
    tanh_one, hidden_one, tanh_two, hidden_two = hidden(w, features)
    pre_two = (dot(w["out_t"][...], out_cot) * (1.0 - tanh_two * tanh_two)).astype(BF16)
    pre_one = (dot(w["mid_t"][...], pre_two) * (1.0 - tanh_one * tanh_one)).astype(BF16)
    feature_cot = dot(w["in_t"][...], pre_one)
    own = to_tiles(feature_cot[0:8, :])
    other = center[:, 0:1] * lam - to_tiles(feature_cot[8:16, :])
    for i, x in enumerate(xs):
        spread.put(x, y, other[i * n : i * n + n])
        direct.put(x, y, own[i * n : i * n + n])
    if sums is None:
        return

    def kept(value):
        if n == OWN_Y:
            return value
        first = [(i * n - y) * LEV for i in range(len(xs))]
        return jnp.concatenate([value[:, k : k + OWN_Y * LEV] for k in first], axis=1)

    kept_one = kept(pre_one)
    kept_two = kept(hidden_two)
    sums[0:128, :] += dot_nt(kept(pre_two), kept(hidden_one))
    sums[128:144, :] += dot_nt(kept(features), kept_one)
    sums[144:160, :] += dot_nt(kept(out_cot), kept_two)
    if emit is not None:
        closure = closure_of(w, kept_two)
        for i, x in enumerate(xs):
            tiles = slice(-y, OWN_Y - y)
            emit(x, centers[i][tiles], slopes[i][tiles], closure[i * OWN_Y : (i + 1) * OWN_Y])


def closure_backward(
    w, fields, lead, x_lo, x_hi, y_lo, y_hi, spread, direct, sums, emit=None, own_group=2, rim_group=2
):
    n = y_hi - y_lo

    def own_x(i, carry):
        xs = [i * own_group + j for j in range(own_group)]
        backward_tiles(w, fields, lead, xs, y_lo, n, spread, direct, sums, emit)
        return carry

    def rim_x(i, carry):
        first = x_lo - 2 + i * rim_group
        first = first + (0 if first < 0 else OWN_X)
        xs = [first + j for j in range(rim_group)]
        backward_tiles(w, fields, lead, xs, y_lo, n, spread, direct, None, None)
        return carry

    repeat(OWN_X // own_group, own_x)
    repeat((x_hi - x_lo + 4 - OWN_X) // rim_group, rim_x)


def adjoint_tiles(fields, lead, x, y, n, spread, direct):
    lam = lead.get(x, y, n)
    up, down = lead.get(x, y + 1, n), lead.get(x, y - 1, n)
    s_up, s_down = fields.get(x, y + 1, n), fields.get(x, y - 1, n)
    laplace = lead.get(x + 1, y, n) + lead.get(x - 1, y, n) + up + down - 4.0 * lam
    result = deriv_x(lambda k: spread.get(x + k, y, n)) + direct.get(x, y, n) + DIFFUSION * laplace
    result = result + 0.5 * (s_up[:, 1:2] * up - s_down[:, 1:2] * down)
    along_x = deriv_x(lambda k: fields.get(x + k, y, n))
    along_y = (s_up - s_down) * 0.5
    to_u = jnp.sum(lam * along_x, axis=1, keepdims=True)
    to_v = jnp.sum(lam * along_y, axis=1, keepdims=True)
    row = lax.broadcasted_iota(jnp.int32, lam.shape, 1)
    return lam, result - jnp.where(row == 0, to_u, 0.0) - jnp.where(row == 1, to_v, 0.0)


def weights_of(bundle):
    return {
        "mid": bundle.at[0:128, :],
        "mid_t": bundle.at[128:256, :],
        "in_t": bundle.at[256:272, :],
        "out": bundle.at[272:288, :],
    }


def split_three(value):
    high = value.astype(BF16)
    rest = value - high.astype(F32)
    middle = rest.astype(BF16)
    return high, middle, (rest - middle.astype(F32)).astype(BF16)


def pick(value, chosen):
    count = value.shape[0]
    parts = dot(jnp.concatenate(split_three(value), axis=0), chosen)
    return parts[0:count] + parts[count : 2 * count] + parts[2 * count : 3 * count]


def first_table():
    table = np.zeros((GZ, LEV), np.int32)
    for block in range(GZ):
        for x in range(OWN_X):
            for y in range(18):
                table[block, x * 18 + y] = x * 64 + (8 * block - 5 + y) % 64
            for y in range(14):
                table[block, 72 + x * 14 + y] = 256 + x * 64 + (8 * block - 3 + y) % 64
    return table


def pack_kernel(table, state, cot, fall, live, out, rates, left, given):
    left[:, 0:256] = state[...].reshape(96, 256)
    left[:, 256:512] = cot[...].reshape(96, 256)
    given[...] = jnp.zeros(given.shape, F32)
    given[0:1, :] = fall[...]
    given[1:2, :] = live[...].astype(F32)
    turn = 32 * turned_half(lax.axis_index("gx"))
    place = lax.broadcasted_iota(jnp.int32, (512, LEV), 0) ^ turn
    parts = jnp.concatenate(split_three(left[...]), axis=0)
    for block in range(GZ):
        chosen = jnp.where(place == table[block : block + 1, :], 1.0, 0.0).astype(BF16)
        wide = dot(parts, chosen)
        out[block] = wide[0:96] + wide[96:192] + wide[192:288]
    mine = table[pl.ds(lax.axis_index("gz"), 1), :]
    chosen = jnp.where(place[0:256] == mine, 1.0, 0.0).astype(BF16)
    rates[...] = pick(given[...], chosen)[0:8]


def turn_kernel(got, rates, to_next, to_prev):
    for which in range(NF):
        blocks = [got[k, which * 16 : which * 16 + 16, :] for k in range(GZ)]
        turned = jnp.concatenate(blocks, axis=0).T
        to_next[which * 72 : which * 72 + 72, :] = turned[0:72]
        to_prev[which * 72 : which * 72 + 72, :] = turned[0:72]
        to_next[432 + which * 28 : 460 + which * 28, :] = turned[100:128]
        to_prev[432 + which * 28 : 460 + which * 28, :] = turned[72:100]
    to_next[600:608, :] = rates[...]
    to_prev[600:608, :] = rates[...]


def forward_kernel(
    own, before, after, bundle, w_in, w_out_t, radiation,
    state, fall, live, one, to_both, next_one, prev_one,
    two, p_theta, p_rain, p_fall, p_live,
):
    w = weights_of(bundle) | {"in": w_in, "out_t": w_out_t}
    packs = (p_theta, p_rain, p_fall, p_live)
    state[...] = jnp.zeros(state.shape, F32)
    for place, source in enumerate((before, own, after)):
        for which in range(NF):
            columns = source[which * 72 : which * 72 + 72, :]
            state[pl.ds(place * 576 + which, 72, stride=8), :] = columns
        rows = pl.ds(place * 72, 72)
        fall[rows, :] = jnp.broadcast_to(source[600:601, :], (LEV, LEV)).T[0:72]
        live[rows, :] = jnp.broadcast_to(source[601:602, :], (LEV, LEV)).T[0:72]
    s_zero = Patch(state, -4, 12, -5, 18)
    s_one = Patch(one, -2, 8, -4, 16)
    s_two = Patch(two, 0, 4, -3, 14)

    def stage_one(i, carry):
        xs = [i * GROUP_ONE - 2 + j for j in range(GROUP_ONE)]
        for x, center, total in forward_tiles(w, s_zero, xs, -4, 16):
            s_one.put(x, -4, center + STEP * total)
        return carry

    repeat(8 // GROUP_ONE, stage_one)
    xs = range(-2, 6)
    column_terms(s_zero, xs, -4, 16, fall, live, radiation, packs, False)
    add_columns(s_one, xs, -4, 16, packs, STEP)

    def stage_two(i, carry):
        xs = [i * GROUP_TWO + j for j in range(GROUP_TWO)]
        for x, center, total in forward_tiles(w, s_one, xs, -3, 14):
            s_two.put(x, -3, 0.75 * s_zero.get(x, -3, 14) + 0.25 * (center + STEP * total))
        return carry

    repeat(4 // GROUP_TWO, stage_two)
    xs = range(4)
    column_terms(s_one, xs, -3, 14, fall, live, radiation, packs, False)
    add_columns(s_two, xs, -3, 14, packs, 0.25 * STEP)
    for which in range(NF):
        to_both[which * 56 : which * 56 + 56, :] = two[pl.ds(which, 56, stride=8), :]
        for i in range(4):
            rows = pl.ds(which * 48 + i * 12, 12)
            next_one[rows, :] = s_one.field(i - 2, -2, 12, which)
            prev_one[rows, :] = s_one.field(i + 2, -2, 12, which)


def middle_kernel(
    own, before, after, cot_before, prev_cot, next_cot, cot_after,
    bundle, w_in, w_out_t, radiation, state, fall, live,
    cot_two, to_both, new_state, known, sums,
    two, lead, spread, direct, p_theta, p_rain, p_fall, p_live,
):
    w = weights_of(bundle) | {"in": w_in, "out_t": w_out_t}
    packs = (p_theta, p_rain, p_fall, p_live)
    two[...] = jnp.zeros(two.shape, F32)
    for place, source in enumerate((before, own, after)):
        for which in range(NF):
            columns = source[which * 56 : which * 56 + 56, :]
            two[pl.ds(place * 448 + which, 56, stride=8), :] = columns
    lead[...] = jnp.zeros(lead.shape, F32)
    for place, source in enumerate((cot_before, prev_cot, next_cot, cot_after)):
        for which in range(NF):
            columns = source[432 + which * 28 : 460 + which * 28, :]
            lead[pl.ds(place * 224 + which, 28, stride=8), :] = (2.0 / 3.0) * columns
    sums[...] = jnp.zeros(sums.shape, F32)
    s_zero = Patch(state, -4, 12, -5, 18)
    s_two = Patch(two, -4, 12, -3, 14)
    lam = Patch(lead, -2, 8, -3, 14)
    spread_at, direct_at = Patch(spread, -2, 8, -2, 12), Patch(direct, -2, 8, -2, 12)
    c_two = Patch(cot_two, 0, 4, -2, 12)
    new = Patch(new_state, 0, 4, 0, 8)

    def emit(x, center, along_x, closure):
        total = moved_of(s_two, x, 0, OWN_Y, center, along_x) + closure
        old = s_zero.get(x, 0, OWN_Y)
        new.put(x, 0, old * (1.0 / 3.0) + (2.0 / 3.0) * (center + STEP * total))

    closure_backward(w, s_two, lam, 0, 4, -2, 10, spread_at, direct_at, sums, emit, *GROUP_B2)
    xs = range(4)
    column_terms(s_two, xs, 0, 8, fall, live, radiation, packs, False)
    add_columns(new, xs, 0, 8, packs, (2.0 / 3.0) * STEP)

    def gather(x, carry):
        center, result = adjoint_tiles(s_two, lam, x, -2, 12, spread_at, direct_at)
        c_two.put(x, -2, center + STEP * result)
        return carry

    repeat(4, gather)
    column_terms(lam, xs, -2, 12, fall, live, radiation, packs, True)
    add_columns(c_two, xs, -2, 12, packs, STEP)
    base = Patch(known, 0, 4, 0, 8)
    for x in xs:
        base.put(x, 0, 0.5 * lam.get(x, 0, 8) + 0.75 * c_two.get(x, 0, 8))
    for which in range(NF):
        to_both[which * 48 : which * 48 + 48, :] = cot_two[pl.ds(which, 48, stride=8), :]


def last_kernel(
    own, before, after, one, one_before, one_after, bundle, w_in, w_out_t, radiation,
    state, fall, live, new_state, known, sums_two,
    out,
    wide, lead, c_one, spread, direct, spread_zero, direct_zero, grad, sums,
    p_theta, p_rain, p_fall, p_live,
):
    w = weights_of(bundle) | {"in": w_in, "out_t": w_out_t}
    packs = (p_theta, p_rain, p_fall, p_live)
    wide[...] = jnp.zeros(wide.shape, F32)
    lead[...] = jnp.zeros(lead.shape, F32)
    for which in range(NF):
        rows = slice(which * 48, which * 48 + 48)
        wide[pl.ds(which, 48, stride=8), :] = one_before[rows, :]
        wide[pl.ds(1152 + which, 48, stride=8), :] = one_after[rows, :]
        lead[pl.ds(which, 48, stride=8), :] = 0.25 * before[rows, :]
        lead[pl.ds(768 + which, 48, stride=8), :] = 0.25 * after[rows, :]
    s_own = Patch(one, -2, 8, -4, 16)
    for i in range(8):
        wide[pl.ds((i + 4) * 96, 96), :] = one[pl.ds(s_own.at(i - 2, -2), 96), :]
    lead[384:768, :] = 0.25 * own[...]
    sums[...] = sums_two[...]
    s_zero = Patch(state, -4, 12, -5, 18)
    s_one = Patch(wide, -6, 16, -2, 12)
    lam_one = Patch(lead, -4, 12, -2, 12)
    lam_zero = Patch(c_one, -2, 8, -1, 10)
    spread_at, direct_at = Patch(spread, -4, 12, -1, 10), Patch(direct, -4, 12, -1, 10)
    closure_backward(w, s_one, lam_one, -2, 6, -1, 9, spread_at, direct_at, sums, None, *GROUP_B1)

    def gather_one(i, carry):
        x = i - 2
        center, result = adjoint_tiles(s_one, lam_one, x, -1, 10, spread_at, direct_at)
        lam_zero.put(x, -1, center + STEP * result)
        return carry

    repeat(8, gather_one)
    xs = range(-2, 6)
    column_terms(lam_one, xs, -1, 10, fall, live, radiation, packs, True)
    add_columns(lam_zero, xs, -1, 10, packs, STEP)

    spread_z, direct_z = Patch(spread_zero, -2, 8, 0, 8), Patch(direct_zero, -2, 8, 0, 8)
    closure_backward(w, s_zero, lam_zero, 0, 4, 0, 8, spread_z, direct_z, sums, None, *GROUP_B0)
    base = Patch(known, 0, 4, 0, 8)
    final = Patch(grad, 0, 4, 0, 8)

    def gather_zero(x, carry):
        center, result = adjoint_tiles(s_zero, lam_zero, x, 0, 8, spread_z, direct_z)
        final.put(x, 0, base.get(x, 0, 8) + center + STEP * result)
        return carry

    repeat(4, gather_zero)
    xs = range(4)
    column_terms(lam_zero, xs, 0, 8, fall, live, radiation, packs, True)
    add_columns(final, xs, 0, 8, packs, STEP)
    for pair in range(3):
        rows = []
        for source in (new_state, grad):
            for which in (2 * pair, 2 * pair + 1):
                rows.append(source[pl.ds(which, 32, stride=8), :])
        turned = jnp.concatenate(rows, axis=0).T
        for block in range(GZ):
            out[block, pair * 16 : pair * 16 + 16, :] = turned[block * 16 : block * 16 + 16]
    for block in range(GZ):
        out[block, 48:68, :] = STEP * sums[block * CHUNK : (block + 1) * CHUNK, :]


def last_table():
    chosen = np.zeros((256, 256), np.float32)
    for block in range(GZ):
        for x in range(OWN_X):
            for y in range(OWN_Y):
                chosen[block * 32 + x * 8 + y, x * 64 + block * 8 + y] = 1.0
    return chosen


def sum_kernel(got, out):
    total = got[0, 48:68, :]
    for block in range(1, GZ):
        total = total + got[block, 48:68, :]
    for slab in range(GX):
        out[slab] = total


def unpack_kernel(got, chosen, new_state, grad):
    turn = 4 * turned_half(lax.axis_index("gx"))
    rows = []
    for part in range(4):
        lanes = slice(part * 32, part * 32 + 32)
        rows.append(jnp.concatenate([got[k ^ turn, 0:48, lanes] for k in range(GZ)], axis=1))
    placed = pick(jnp.concatenate(rows, axis=0), chosen[...])
    for part in range(4):
        for pair in range(3):
            first = part * 48 + pair * 16
            out = (new_state, grad)[part // 2]
            out[2 * pair + part % 2] = placed[first : first + 16]


def finish_kernel(got, grad_in, grad_mid, grad_out):
    total = got[...].reshape(GZ * CHUNK, LEV)
    grad_mid[...] = total[0:128]
    rows = [total[128:134], total[136:142], jnp.zeros((116, LEV), F32)]
    grad_in[...] = jnp.concatenate(rows, axis=0).T[:, 0:12]
    grad_out[...] = total[144:150]


def call(kernel, outs, scratch, *operands, giga=0):
    vmem = pl.BlockSpec(memory_space=pltpu.VMEM)
    return pl.pallas_call(
        kernel,
        out_shape=[jax.ShapeDtypeStruct(shape, F32) for shape in outs],
        in_specs=[vmem] * len(operands),
        out_specs=[vmem] * len(outs),
        scratch_shapes=[pltpu.VMEM(shape, F32) for shape in scratch],
        cost_estimate=pl.CostEstimate(flops=giga * 10**9, transcendentals=0, bytes_accessed=10**6)
        if giga
        else None,
        compiler_params=pltpu.CompilerParams(vmem_limit_bytes=48 << 20),
    )(*operands)


def turned_half(slab):
    return (slab // 4) % 2


def passed_along(shard, by):
    pairs = []
    for block in range(GZ):
        for slab in range(GX):
            other = (slab + by) % GX
            place = block ^ (4 * (turned_half(slab) ^ turned_half(other)))
            pairs.append((block * GX + slab, place * GX + other))
    return lax.ppermute(shard, ("gz", "gx"), pairs)


def on_device(state, state_cot, w_in, w_mid, w_out, radiation, fall_rate, active):
    packs = [(8 * PACK, LEV)] * 4
    in_wide = jnp.concatenate(
        [jnp.pad(w_in[:, :NF], ((0, 0), (0, 2))), jnp.pad(w_in[:, NF:], ((0, 0), (0, 2)))], axis=1
    )
    out_wide = jnp.pad(w_out, ((0, 10), (0, 0)))
    bundle = jnp.concatenate([w_mid, w_mid.T, in_wide.T, out_wide], axis=0)
    weights = (bundle, in_wide, out_wide.T, radiation)

    packed, rates = call(
        pack_kernel,
        [(GZ, 96, LEV), (8, LEV)],
        [(96, 512), (16, 256)],
        jnp.asarray(first_table()),
        state,
        state_cot,
        fall_rate.reshape(1, 256),
        active.reshape(1, 256),
    )
    got = lax.all_to_all(packed, "gz", 0, 0)
    own, own_prev = call(turn_kernel, [(608, LEV), (608, LEV)], [], got, rates)
    before, after = passed_along(own, 1), passed_along(own_prev, -1)
    zero, fall, live, one, two, next_one, prev_one = call(
        forward_kernel,
        [(1728, LEV), (216, LEV), (216, LEV), (1024, LEV), (336, LEV), (288, LEV), (288, LEV)],
        [(448, LEV)] + packs,
        own,
        before,
        after,
        *weights,
        giga=12,
    )
    two_before, two_after = passed_along(two, 1), passed_along(two, -1)
    one_before, one_after = passed_along(next_one, 1), passed_along(prev_one, -1)
    cot_two, to_both, new_state, known, sums = call(
        middle_kernel,
        [(384, LEV), (288, LEV), (256, LEV), (256, LEV), (GZ * CHUNK, LEV)],
        [(1344, LEV), (896, LEV), (768, LEV), (768, LEV)] + packs,
        two,
        two_before,
        two_after,
        before,
        own_prev,
        own,
        after,
        *weights,
        zero,
        fall,
        live,
        giga=11,
    )
    lead_before, lead_after = passed_along(to_both, 1), passed_along(to_both, -1)
    (sent,) = call(
        last_kernel,
        [(GZ, 68, LEV)],
        [(1536, LEV), (1152, LEV), (640, LEV), (960, LEV), (960, LEV), (512, LEV), (512, LEV)]
        + [(256, LEV), (GZ * CHUNK, LEV)]
        + packs,
        cot_two,
        lead_before,
        lead_after,
        one,
        one_before,
        one_after,
        *weights,
        zero,
        fall,
        live,
        new_state,
        known,
        sums,
        giga=20,
    )
    got = lax.all_to_all(sent, "gz", 0, 0)
    (chunks,) = call(sum_kernel, [(GX, CHUNK, LEV)], [], got)
    new_state, grad_state = call(
        unpack_kernel,
        [(NF, 16, 256), (NF, 16, 256)],
        [],
        got,
        jnp.asarray(last_table(), BF16),
    )
    spread = lax.all_to_all(chunks, "gx", 0, 0)
    added = jnp.sum(spread, axis=0)
    totals = lax.all_to_all(jnp.broadcast_to(added, (GZ, CHUNK, LEV)), "gz", 0, 0)
    grads = call(finish_kernel, [(128, 2 * NF), (128, LEV), (NF, LEV)], [], totals)
    return (new_state, grad_state, *grads)


def solution(mesh):
    placed = (P(None, "gz", "gx"), P(None, "gz", "gx"), P(), P(), P(), P(), P("gx"), P("gx"))
    return jax.shard_map(
        on_device,
        mesh=mesh,
        in_specs=placed,
        out_specs=(P(None, "gz", "gx"), P(None, "gz", "gx"), P(), P(), P()),
        check_vma=False,
    )
```

```python
import jax
import jax.numpy as jnp
import numpy as np
from jax import lax
from jax.experimental import pallas as pl
from jax.experimental.pallas import tpu as pltpu
from jax.sharding import PartitionSpec as P

NF = 6
LEV = 128
OWN_X = 4
OWN_Y = 8
GZ = 8
GX = 32
DIFFUSION = 0.1
STEP = 0.25
F32 = jnp.float32
BF16 = jnp.bfloat16
HIGHEST = lax.Precision.HIGHEST
CHUNK = 20
GROUP_ONE, GROUP_TWO = 8, 4
GROUP_B2, GROUP_B1, GROUP_B0 = (4, 2), (4, 4), (4, 2)
PACK = 16


class Patch:
    def __init__(self, ref, x0, nx, y0, ny):
        self.ref, self.x0, self.nx, self.y0, self.ny = ref, x0, nx, y0, ny

    def at(self, x, y):
        start = ((x - self.x0) * self.ny + (y - self.y0)) * 8
        return start if isinstance(start, int) else pl.multiple_of(start, 8)

    def get(self, x, y, n):
        return self.ref[pl.ds(self.at(x, y), n * 8), :].reshape(n, 8, LEV)

    def put(self, x, y, value):
        n = value.shape[0]
        self.ref[pl.ds(self.at(x, y), n * 8), :] = value.reshape(n * 8, LEV)

    def field(self, x, y, n, which):
        return self.ref[pl.ds(self.at(x, y) + which, n, stride=8), :]

    def add_field(self, x, y, which, value):
        n = value.shape[0]
        place = pl.ds(self.at(x, y) + which, n, stride=8)
        self.ref[place, :] = self.ref[place, :] + value


def repeat(count, body):
    for i in range(count):
        body(i, 0)


def dot(a, b):
    return lax.dot_general(a, b, (((1,), (0,)), ((), ())), preferred_element_type=F32)


def dot_nt(a, b):
    return lax.dot_general(a, b, (((1,), (1,)), ((), ())), preferred_element_type=F32)


def to_lanes(tiles):
    return jnp.concatenate([tiles[i] for i in range(tiles.shape[0])], axis=1)


def to_tiles(wide):
    count = wide.shape[1] // LEV
    return jnp.concatenate([wide[None, :, i * LEV : (i + 1) * LEV] for i in range(count)], axis=0)


def deriv_x(get):
    return (8.0 * (get(1) - get(-1)) - (get(2) - get(-2))) * (1.0 / 12.0)


def features_of(center, along_x):
    return to_lanes(jnp.concatenate([center, along_x], axis=1).astype(BF16))


def hidden(w, features):
    tanh_one = jnp.tanh(dot(w["in"][...], features))
    hidden_one = tanh_one.astype(BF16)
    tanh_two = jnp.tanh(dot(w["mid"][...], hidden_one))
    return tanh_one, hidden_one, tanh_two, tanh_two.astype(BF16)


def closure_of(w, hidden_two):
    return to_tiles(dot(w["out"][...], hidden_two)[:8, :])


def moved_of(fields, x, y, n, center, along_x):
    y_plus, y_minus = fields.get(x, y + 1, n), fields.get(x, y - 1, n)
    x_sum = fields.get(x + 1, y, n) + fields.get(x - 1, y, n)
    along_y = (y_plus - y_minus) * 0.5
    laplace = x_sum + y_plus + y_minus - 4.0 * center
    return -(center[:, 0:1] * along_x + center[:, 1:2] * along_y) + DIFFUSION * laplace


def joined(parts):
    return jnp.concatenate(parts, axis=0) if len(parts) > 1 else parts[0]


def forward_tiles(w, fields, xs, y, n):
    centers = [fields.get(x, y, n) for x in xs]
    slopes = [deriv_x(lambda k, x=x: fields.get(x + k, y, n)) for x in xs]
    closure = closure_of(w, hidden(w, features_of(joined(centers), joined(slopes)))[3])
    result = []
    for i, x in enumerate(xs):
        moved = moved_of(fields, x, y, n, centers[i], slopes[i])
        result.append((x, centers[i], moved + closure[i * n : i * n + n]))
    return result


def shifted(value, by):
    lane = lax.broadcasted_iota(jnp.int32, value.shape, 1)
    if by > 0:
        return jnp.where(lane >= by, pltpu.roll(value, by, 1), 0.0)
    return jnp.where(lane < LEV + by, pltpu.roll(value, LEV + by, 1), 0.0)


def settle(source, fall_rate, sign):
    fresh = 1.0 / (1.0 + fall_rate)
    factor = fall_rate * fresh
    value = fresh * source
    step = 1
    while step < LEV:
        value = value + factor * shifted(value, sign * step)
        factor = factor * factor
        step *= 2
    return value


def column_terms(patch, xs, y, n, fall, live, radiation, packs, adjoint):
    p_theta, p_rain, p_fall, p_live = packs
    for i, x in enumerate(xs):
        rows = pl.ds(i * PACK, n)
        p_theta[rows, :] = patch.field(x, y, n, 3)
        p_rain[rows, :] = patch.field(x, y, n, 5)
        source = pl.ds((x + 4) * 18 + y + 5, n)
        p_fall[rows, :] = fall[source, :]
        p_live[rows, :] = live[source, :]
    size = len(xs) * PACK
    theta, rain = p_theta[0:size, :], p_rain[0:size, :]
    fall_rate, mask = p_fall[0:size, :], p_live[0:size, :]
    contract = ((1,), (0,)) if adjoint else ((1,), (1,))
    p_theta[0:size, :] = lax.dot_general(
        theta, radiation[...], (contract, ((), ())), precision=HIGHEST, preferred_element_type=F32
    )
    if adjoint:
        masked = mask * rain
        p_rain[0:size, :] = settle(masked, fall_rate, 1) - masked
    else:
        p_rain[0:size, :] = mask * (settle(rain, fall_rate, -1) - rain)


def add_columns(patch, xs, y, n, packs, gain):
    for i, x in enumerate(xs):
        patch.add_field(x, y, 3, gain * packs[0][pl.ds(i * PACK, n), :])
        patch.add_field(x, y, 5, gain * packs[1][pl.ds(i * PACK, n), :])


def backward_tiles(w, fields, lead, xs, y, n, spread, direct, sums, emit):
    centers = [fields.get(x, y, n) for x in xs]
    slopes = [deriv_x(lambda k, x=x: fields.get(x + k, y, n)) for x in xs]
    center, lam = joined(centers), joined([lead.get(x, y, n) for x in xs])
    features = features_of(center, joined(slopes))
    out_cot = to_lanes(jnp.concatenate([lam, jnp.zeros_like(lam)], axis=1).astype(BF16))
    tanh_one, hidden_one, tanh_two, hidden_two = hidden(w, features)
    pre_two = (dot(w["out_t"][...], out_cot) * (1.0 - tanh_two * tanh_two)).astype(BF16)
    pre_one = (dot(w["mid_t"][...], pre_two) * (1.0 - tanh_one * tanh_one)).astype(BF16)
    feature_cot = dot(w["in_t"][...], pre_one)
    own = to_tiles(feature_cot[0:8, :])
    other = center[:, 0:1] * lam - to_tiles(feature_cot[8:16, :])
    for i, x in enumerate(xs):
        spread.put(x, y, other[i * n : i * n + n])
        direct.put(x, y, own[i * n : i * n + n])
    if sums is None:
        return

    def kept(value):
        if n == OWN_Y:
            return value
        first = [(i * n - y) * LEV for i in range(len(xs))]
        return jnp.concatenate([value[:, k : k + OWN_Y * LEV] for k in first], axis=1)

    kept_one = kept(pre_one)
    kept_two = kept(hidden_two)
    sums[0:128, :] += dot_nt(kept(pre_two), kept(hidden_one))
    sums[128:144, :] += dot_nt(kept(features), kept_one)
    sums[144:160, :] += dot_nt(kept(out_cot), kept_two)
    if emit is not None:
        closure = closure_of(w, kept_two)
        for i, x in enumerate(xs):
            tiles = slice(-y, OWN_Y - y)
            emit(x, centers[i][tiles], slopes[i][tiles], closure[i * OWN_Y : (i + 1) * OWN_Y])


def closure_backward(
    w, fields, lead, x_lo, x_hi, y_lo, y_hi, spread, direct, sums, emit=None, own_group=2, rim_group=2
):
    n = y_hi - y_lo

    def own_x(i, carry):
        xs = [i * own_group + j for j in range(own_group)]
        backward_tiles(w, fields, lead, xs, y_lo, n, spread, direct, sums, emit)
        return carry

    def rim_x(i, carry):
        first = x_lo - 2 + i * rim_group
        first = first + (0 if first < 0 else OWN_X)
        xs = [first + j for j in range(rim_group)]
        backward_tiles(w, fields, lead, xs, y_lo, n, spread, direct, None, None)
        return carry

    repeat(OWN_X // own_group, own_x)
    repeat((x_hi - x_lo + 4 - OWN_X) // rim_group, rim_x)


def adjoint_tiles(fields, lead, x, y, n, spread, direct):
    lam = lead.get(x, y, n)
    up, down = lead.get(x, y + 1, n), lead.get(x, y - 1, n)
    s_up, s_down = fields.get(x, y + 1, n), fields.get(x, y - 1, n)
    laplace = lead.get(x + 1, y, n) + lead.get(x - 1, y, n) + up + down - 4.0 * lam
    result = deriv_x(lambda k: spread.get(x + k, y, n)) + direct.get(x, y, n) + DIFFUSION * laplace
    result = result + 0.5 * (s_up[:, 1:2] * up - s_down[:, 1:2] * down)
    along_x = deriv_x(lambda k: fields.get(x + k, y, n))
    along_y = (s_up - s_down) * 0.5
    to_u = jnp.sum(lam * along_x, axis=1, keepdims=True)
    to_v = jnp.sum(lam * along_y, axis=1, keepdims=True)
    row = lax.broadcasted_iota(jnp.int32, lam.shape, 1)
    return lam, result - jnp.where(row == 0, to_u, 0.0) - jnp.where(row == 1, to_v, 0.0)


def weights_of(bundle):
    return {
        "mid": bundle.at[0:128, :],
        "mid_t": bundle.at[128:256, :],
        "in_t": bundle.at[256:272, :],
        "out": bundle.at[272:288, :],
    }


def split_three(value):
    high = value.astype(BF16)
    rest = value - high.astype(F32)
    middle = rest.astype(BF16)
    return high, middle, (rest - middle.astype(F32)).astype(BF16)


def pick(value, chosen):
    count = value.shape[0]
    parts = dot(jnp.concatenate(split_three(value), axis=0), chosen)
    return parts[0:count] + parts[count : 2 * count] + parts[2 * count : 3 * count]


def first_table():
    table = np.zeros((GZ, LEV), np.int32)
    for block in range(GZ):
        for x in range(OWN_X):
            for y in range(18):
                table[block, x * 18 + y] = x * 64 + (8 * block - 5 + y) % 64
            for y in range(14):
                table[block, 72 + x * 14 + y] = 256 + x * 64 + (8 * block - 3 + y) % 64
    return table


def pack_kernel(table, state, cot, fall, live, out, rates, left, given):
    left[:, 0:256] = state[...].reshape(96, 256)
    left[:, 256:512] = cot[...].reshape(96, 256)
    given[...] = jnp.zeros(given.shape, F32)
    given[0:1, :] = fall[...]
    given[1:2, :] = live[...].astype(F32)
    turn = 32 * turned_half(lax.axis_index("gx"))
    place = lax.broadcasted_iota(jnp.int32, (512, LEV), 0) ^ turn
    parts = jnp.concatenate(split_three(left[...]), axis=0)
    for block in range(GZ):
        chosen = jnp.where(place == table[block : block + 1, :], 1.0, 0.0).astype(BF16)
        wide = dot(parts, chosen)
        out[block] = wide[0:96] + wide[96:192] + wide[192:288]
    mine = table[pl.ds(lax.axis_index("gz"), 1), :]
    chosen = jnp.where(place[0:256] == mine, 1.0, 0.0).astype(BF16)
    rates[...] = pick(given[...], chosen)[0:8]


def turn_kernel(got, rates, to_next, to_prev):
    for which in range(NF):
        blocks = [got[k, which * 16 : which * 16 + 16, :] for k in range(GZ)]
        turned = jnp.concatenate(blocks, axis=0).T
        to_next[which * 72 : which * 72 + 72, :] = turned[0:72]
        to_prev[which * 72 : which * 72 + 72, :] = turned[0:72]
        to_next[432 + which * 28 : 460 + which * 28, :] = turned[100:128]
        to_prev[432 + which * 28 : 460 + which * 28, :] = turned[72:100]
    to_next[600:608, :] = rates[...]
    to_prev[600:608, :] = rates[...]


def forward_kernel(
    own, before, after, bundle, w_in, w_out_t, radiation,
    state, fall, live, one, to_both, next_one, prev_one,
    two, p_theta, p_rain, p_fall, p_live,
):
    w = weights_of(bundle) | {"in": w_in, "out_t": w_out_t}
    packs = (p_theta, p_rain, p_fall, p_live)
    state[...] = jnp.zeros(state.shape, F32)
    for place, source in enumerate((before, own, after)):
        for which in range(NF):
            columns = source[which * 72 : which * 72 + 72, :]
            state[pl.ds(place * 576 + which, 72, stride=8), :] = columns
        rows = pl.ds(place * 72, 72)
        fall[rows, :] = jnp.broadcast_to(source[600:601, :], (LEV, LEV)).T[0:72]
        live[rows, :] = jnp.broadcast_to(source[601:602, :], (LEV, LEV)).T[0:72]
    s_zero = Patch(state, -4, 12, -5, 18)
    s_one = Patch(one, -2, 8, -4, 16)
    s_two = Patch(two, 0, 4, -3, 14)

    def stage_one(i, carry):
        xs = [i * GROUP_ONE - 2 + j for j in range(GROUP_ONE)]
        for x, center, total in forward_tiles(w, s_zero, xs, -4, 16):
            s_one.put(x, -4, center + STEP * total)
        return carry

    repeat(8 // GROUP_ONE, stage_one)
    xs = range(-2, 6)
    column_terms(s_zero, xs, -4, 16, fall, live, radiation, packs, False)
    add_columns(s_one, xs, -4, 16, packs, STEP)

    def stage_two(i, carry):
        xs = [i * GROUP_TWO + j for j in range(GROUP_TWO)]
        for x, center, total in forward_tiles(w, s_one, xs, -3, 14):
            s_two.put(x, -3, 0.75 * s_zero.get(x, -3, 14) + 0.25 * (center + STEP * total))
        return carry

    repeat(4 // GROUP_TWO, stage_two)
    xs = range(4)
    column_terms(s_one, xs, -3, 14, fall, live, radiation, packs, False)
    add_columns(s_two, xs, -3, 14, packs, 0.25 * STEP)
    for which in range(NF):
        to_both[which * 56 : which * 56 + 56, :] = two[pl.ds(which, 56, stride=8), :]
        for i in range(4):
            rows = pl.ds(which * 48 + i * 12, 12)
            next_one[rows, :] = s_one.field(i - 2, -2, 12, which)
            prev_one[rows, :] = s_one.field(i + 2, -2, 12, which)


def middle_kernel(
    own, before, after, cot_before, prev_cot, next_cot, cot_after,
    bundle, w_in, w_out_t, radiation, state, fall, live,
    cot_two, to_both, new_state, known, sums,
    two, lead, spread, direct, p_theta, p_rain, p_fall, p_live,
):
    w = weights_of(bundle) | {"in": w_in, "out_t": w_out_t}
    packs = (p_theta, p_rain, p_fall, p_live)
    two[...] = jnp.zeros(two.shape, F32)
    for place, source in enumerate((before, own, after)):
        for which in range(NF):
            columns = source[which * 56 : which * 56 + 56, :]
            two[pl.ds(place * 448 + which, 56, stride=8), :] = columns
    lead[...] = jnp.zeros(lead.shape, F32)
    for place, source in enumerate((cot_before, prev_cot, next_cot, cot_after)):
        for which in range(NF):
            columns = source[432 + which * 28 : 460 + which * 28, :]
            lead[pl.ds(place * 224 + which, 28, stride=8), :] = (2.0 / 3.0) * columns
    sums[...] = jnp.zeros(sums.shape, F32)
    s_zero = Patch(state, -4, 12, -5, 18)
    s_two = Patch(two, -4, 12, -3, 14)
    lam = Patch(lead, -2, 8, -3, 14)
    spread_at, direct_at = Patch(spread, -2, 8, -2, 12), Patch(direct, -2, 8, -2, 12)
    c_two = Patch(cot_two, 0, 4, -2, 12)
    new = Patch(new_state, 0, 4, 0, 8)

    def emit(x, center, along_x, closure):
        total = moved_of(s_two, x, 0, OWN_Y, center, along_x) + closure
        old = s_zero.get(x, 0, OWN_Y)
        new.put(x, 0, old * (1.0 / 3.0) + (2.0 / 3.0) * (center + STEP * total))

    closure_backward(w, s_two, lam, 0, 4, -2, 10, spread_at, direct_at, sums, emit, *GROUP_B2)
    xs = range(4)
    column_terms(s_two, xs, 0, 8, fall, live, radiation, packs, False)
    add_columns(new, xs, 0, 8, packs, (2.0 / 3.0) * STEP)

    def gather(x, carry):
        center, result = adjoint_tiles(s_two, lam, x, -2, 12, spread_at, direct_at)
        c_two.put(x, -2, center + STEP * result)
        return carry

    repeat(4, gather)
    column_terms(lam, xs, -2, 12, fall, live, radiation, packs, True)
    add_columns(c_two, xs, -2, 12, packs, STEP)
    base = Patch(known, 0, 4, 0, 8)
    for x in xs:
        base.put(x, 0, 0.5 * lam.get(x, 0, 8) + 0.75 * c_two.get(x, 0, 8))
    for which in range(NF):
        to_both[which * 48 : which * 48 + 48, :] = cot_two[pl.ds(which, 48, stride=8), :]


def last_kernel(
    own, before, after, one, one_before, one_after, bundle, w_in, w_out_t, radiation,
    state, fall, live, new_state, known, sums_two,
    out,
    wide, lead, c_one, spread, direct, spread_zero, direct_zero, grad, sums,
    p_theta, p_rain, p_fall, p_live,
):
    w = weights_of(bundle) | {"in": w_in, "out_t": w_out_t}
    packs = (p_theta, p_rain, p_fall, p_live)
    wide[...] = jnp.zeros(wide.shape, F32)
    lead[...] = jnp.zeros(lead.shape, F32)
    for which in range(NF):
        rows = slice(which * 48, which * 48 + 48)
        wide[pl.ds(which, 48, stride=8), :] = one_before[rows, :]
        wide[pl.ds(1152 + which, 48, stride=8), :] = one_after[rows, :]
        lead[pl.ds(which, 48, stride=8), :] = 0.25 * before[rows, :]
        lead[pl.ds(768 + which, 48, stride=8), :] = 0.25 * after[rows, :]
    s_own = Patch(one, -2, 8, -4, 16)
    for i in range(8):
        wide[pl.ds((i + 4) * 96, 96), :] = one[pl.ds(s_own.at(i - 2, -2), 96), :]
    lead[384:768, :] = 0.25 * own[...]
    sums[...] = sums_two[...]
    s_zero = Patch(state, -4, 12, -5, 18)
    s_one = Patch(wide, -6, 16, -2, 12)
    lam_one = Patch(lead, -4, 12, -2, 12)
    lam_zero = Patch(c_one, -2, 8, -1, 10)
    spread_at, direct_at = Patch(spread, -4, 12, -1, 10), Patch(direct, -4, 12, -1, 10)
    closure_backward(w, s_one, lam_one, -2, 6, -1, 9, spread_at, direct_at, sums, None, *GROUP_B1)

    def gather_one(i, carry):
        x = i - 2
        center, result = adjoint_tiles(s_one, lam_one, x, -1, 10, spread_at, direct_at)
        lam_zero.put(x, -1, center + STEP * result)
        return carry

    repeat(8, gather_one)
    xs = range(-2, 6)
    column_terms(lam_one, xs, -1, 10, fall, live, radiation, packs, True)
    add_columns(lam_zero, xs, -1, 10, packs, STEP)

    spread_z, direct_z = Patch(spread_zero, -2, 8, 0, 8), Patch(direct_zero, -2, 8, 0, 8)
    closure_backward(w, s_zero, lam_zero, 0, 4, 0, 8, spread_z, direct_z, sums, None, *GROUP_B0)
    base = Patch(known, 0, 4, 0, 8)
    final = Patch(grad, 0, 4, 0, 8)

    def gather_zero(x, carry):
        center, result = adjoint_tiles(s_zero, lam_zero, x, 0, 8, spread_z, direct_z)
        final.put(x, 0, base.get(x, 0, 8) + center + STEP * result)
        return carry

    repeat(4, gather_zero)
    xs = range(4)
    column_terms(lam_zero, xs, 0, 8, fall, live, radiation, packs, True)
    add_columns(final, xs, 0, 8, packs, STEP)
    for pair in range(3):
        rows = []
        for source in (new_state, grad):
            for which in (2 * pair, 2 * pair + 1):
                rows.append(source[pl.ds(which, 32, stride=8), :])
        turned = jnp.concatenate(rows, axis=0).T
        for block in range(GZ):
            out[block, pair * 16 : pair * 16 + 16, :] = turned[block * 16 : block * 16 + 16]
    for block in range(GZ):
        out[block, 48:68, :] = STEP * sums[block * CHUNK : (block + 1) * CHUNK, :]


def last_table():
    chosen = np.zeros((256, 256), np.float32)
    for block in range(GZ):
        for x in range(OWN_X):
            for y in range(OWN_Y):
                chosen[block * 32 + x * 8 + y, x * 64 + block * 8 + y] = 1.0
    return chosen


def sum_kernel(got, out):
    total = got[0, 48:68, :]
    for block in range(1, GZ):
        total = total + got[block, 48:68, :]
    for other in range(out.shape[0]):
        out[other] = total


def unpack_kernel(got, chosen, new_state, grad):
    turn = 4 * turned_half(lax.axis_index("gx"))
    rows = []
    for part in range(4):
        lanes = slice(part * 32, part * 32 + 32)
        rows.append(jnp.concatenate([got[k ^ turn, 0:48, lanes] for k in range(GZ)], axis=1))
    placed = pick(jnp.concatenate(rows, axis=0), chosen[...])
    for part in range(4):
        for pair in range(3):
            first = part * 48 + pair * 16
            out = (new_state, grad)[part // 2]
            out[2 * pair + part % 2] = placed[first : first + 16]


def finish_kernel(got, grad_in, grad_mid, grad_out):
    total = (got[0:GZ] + got[GZ : 2 * GZ]).reshape(GZ * CHUNK, LEV)
    grad_mid[...] = total[0:128]
    rows = [total[128:134], total[136:142], jnp.zeros((116, LEV), F32)]
    grad_in[...] = jnp.concatenate(rows, axis=0).T[:, 0:12]
    grad_out[...] = total[144:150]


def call(kernel, outs, scratch, *operands, giga=0):
    vmem = pl.BlockSpec(memory_space=pltpu.VMEM)
    return pl.pallas_call(
        kernel,
        out_shape=[jax.ShapeDtypeStruct(shape, F32) for shape in outs],
        in_specs=[vmem] * len(operands),
        out_specs=[vmem] * len(outs),
        scratch_shapes=[pltpu.VMEM(shape, F32) for shape in scratch],
        cost_estimate=pl.CostEstimate(flops=giga * 10**9, transcendentals=0, bytes_accessed=10**6)
        if giga
        else None,
        compiler_params=pltpu.CompilerParams(vmem_limit_bytes=48 << 20),
    )(*operands)


def turned_half(slab):
    return (slab // 4) % 2


def passed_along(shard, by):
    pairs = []
    for block in range(GZ):
        for slab in range(GX):
            other = (slab + by) % GX
            place = block ^ (4 * (turned_half(slab) ^ turned_half(other)))
            pairs.append((block * GX + slab, place * GX + other))
    return lax.ppermute(shard, ("gz", "gx"), pairs)


def on_device(state, state_cot, w_in, w_mid, w_out, radiation, fall_rate, active):
    packs = [(8 * PACK, LEV)] * 4
    in_wide = jnp.concatenate(
        [jnp.pad(w_in[:, :NF], ((0, 0), (0, 2))), jnp.pad(w_in[:, NF:], ((0, 0), (0, 2)))], axis=1
    )
    out_wide = jnp.pad(w_out, ((0, 10), (0, 0)))
    bundle = jnp.concatenate([w_mid, w_mid.T, in_wide.T, out_wide], axis=0)
    weights = (bundle, in_wide, out_wide.T, radiation)

    packed, rates = call(
        pack_kernel,
        [(GZ, 96, LEV), (8, LEV)],
        [(96, 512), (16, 256)],
        jnp.asarray(first_table()),
        state,
        state_cot,
        fall_rate.reshape(1, 256),
        active.reshape(1, 256),
    )
    got = lax.all_to_all(packed, "gz", 0, 0)
    own, own_prev = call(turn_kernel, [(608, LEV), (608, LEV)], [], got, rates)
    before, after = passed_along(own, 1), passed_along(own_prev, -1)
    zero, fall, live, one, two, next_one, prev_one = call(
        forward_kernel,
        [(1728, LEV), (216, LEV), (216, LEV), (1024, LEV), (336, LEV), (288, LEV), (288, LEV)],
        [(448, LEV)] + packs,
        own,
        before,
        after,
        *weights,
        giga=12,
    )
    two_before, two_after = passed_along(two, 1), passed_along(two, -1)
    one_before, one_after = passed_along(next_one, 1), passed_along(prev_one, -1)
    cot_two, to_both, new_state, known, sums = call(
        middle_kernel,
        [(384, LEV), (288, LEV), (256, LEV), (256, LEV), (GZ * CHUNK, LEV)],
        [(1344, LEV), (896, LEV), (768, LEV), (768, LEV)] + packs,
        two,
        two_before,
        two_after,
        before,
        own_prev,
        own,
        after,
        *weights,
        zero,
        fall,
        live,
        giga=11,
    )
    lead_before, lead_after = passed_along(to_both, 1), passed_along(to_both, -1)
    (sent,) = call(
        last_kernel,
        [(GZ, 68, LEV)],
        [(1536, LEV), (1152, LEV), (640, LEV), (960, LEV), (960, LEV), (512, LEV), (512, LEV)]
        + [(256, LEV), (GZ * CHUNK, LEV)]
        + packs,
        cot_two,
        lead_before,
        lead_after,
        one,
        one_before,
        one_after,
        *weights,
        zero,
        fall,
        live,
        new_state,
        known,
        sums,
        giga=20,
    )
    got = lax.all_to_all(sent, "gz", 0, 0)
    (chunks,) = call(sum_kernel, [(16, CHUNK, LEV)], [], got)
    new_state, grad_state = call(
        unpack_kernel,
        [(NF, 16, 256), (NF, 16, 256)],
        [],
        got,
        jnp.asarray(last_table(), BF16),
    )
    level = [[8 * x + 4 * half + y for x in range(4) for y in range(4)] for half in range(2)]
    line = [
        [block * GX + 8 * x + 4 * half + y for half in range(2) for block in range(GZ)]
        for x in range(4)
        for y in range(4)
    ]
    added = jnp.sum(lax.all_to_all(chunks, "gx", 0, 0, axis_index_groups=level), axis=0)
    added = jnp.broadcast_to(added, (16, CHUNK, LEV))
    totals = lax.all_to_all(added, ("gz", "gx"), 0, 0, axis_index_groups=line)
    grads = call(finish_kernel, [(128, 2 * NF), (128, LEV), (NF, LEV)], [], totals)
    return (new_state, grad_state, *grads)


def solution(mesh):
    placed = (P(None, "gz", "gx"), P(None, "gz", "gx"), P(), P(), P(), P(), P("gx"), P("gx"))
    return jax.shard_map(
        on_device,
        mesh=mesh,
        in_specs=placed,
        out_specs=(P(None, "gz", "gx"), P(None, "gz", "gx"), P(), P(), P()),
        check_vma=False,
    )
```

```python
import jax
import jax.numpy as jnp
import numpy as np
from jax import lax
from jax.experimental import pallas as pl
from jax.experimental.pallas import tpu as pltpu
from jax.sharding import PartitionSpec as P

NF = 6
LEV = 128
OWN_X = 4
OWN_Y = 8
GZ = 8
GX = 32
DIFFUSION = 0.1
STEP = 0.25
F32 = jnp.float32
BF16 = jnp.bfloat16
HIGHEST = lax.Precision.HIGHEST
CHUNK = 20
GROUP_ONE, GROUP_TWO = 8, 4
GROUP_B2, GROUP_B1, GROUP_B0 = (4, 2), (4, 4), (4, 2)
PACK = 16


class Patch:
    def __init__(self, ref, x0, nx, y0, ny):
        self.ref, self.x0, self.nx, self.y0, self.ny = ref, x0, nx, y0, ny

    def at(self, x, y):
        start = ((x - self.x0) * self.ny + (y - self.y0)) * 8
        return start if isinstance(start, int) else pl.multiple_of(start, 8)

    def get(self, x, y, n):
        return self.ref[pl.ds(self.at(x, y), n * 8), :].reshape(n, 8, LEV)

    def put(self, x, y, value):
        n = value.shape[0]
        self.ref[pl.ds(self.at(x, y), n * 8), :] = value.reshape(n * 8, LEV)

    def field(self, x, y, n, which):
        return self.ref[pl.ds(self.at(x, y) + which, n, stride=8), :]

    def add_field(self, x, y, which, value):
        n = value.shape[0]
        place = pl.ds(self.at(x, y) + which, n, stride=8)
        self.ref[place, :] = self.ref[place, :] + value


def repeat(count, body):
    for i in range(count):
        body(i, 0)


def dot(a, b):
    return lax.dot_general(a, b, (((1,), (0,)), ((), ())), preferred_element_type=F32)


def dot_nt(a, b):
    return lax.dot_general(a, b, (((1,), (1,)), ((), ())), preferred_element_type=F32)


def to_lanes(tiles):
    return jnp.concatenate([tiles[i] for i in range(tiles.shape[0])], axis=1)


def to_tiles(wide):
    count = wide.shape[1] // LEV
    return jnp.concatenate([wide[None, :, i * LEV : (i + 1) * LEV] for i in range(count)], axis=0)


def deriv_x(get):
    return (8.0 * (get(1) - get(-1)) - (get(2) - get(-2))) * (1.0 / 12.0)


def features_of(center, along_x):
    return to_lanes(jnp.concatenate([center, along_x], axis=1).astype(BF16))


def hidden(w, features):
    tanh_one = jnp.tanh(dot(w["in"][...], features))
    hidden_one = tanh_one.astype(BF16)
    tanh_two = jnp.tanh(dot(w["mid"][...], hidden_one))
    return tanh_one, hidden_one, tanh_two, tanh_two.astype(BF16)


def closure_of(w, hidden_two):
    return to_tiles(dot(w["out"][...], hidden_two)[:8, :])


def moved_of(fields, x, y, n, center, along_x):
    y_plus, y_minus = fields.get(x, y + 1, n), fields.get(x, y - 1, n)
    x_sum = fields.get(x + 1, y, n) + fields.get(x - 1, y, n)
    along_y = (y_plus - y_minus) * 0.5
    laplace = x_sum + y_plus + y_minus - 4.0 * center
    return -(center[:, 0:1] * along_x + center[:, 1:2] * along_y) + DIFFUSION * laplace


def joined(parts):
    return jnp.concatenate(parts, axis=0) if len(parts) > 1 else parts[0]


def forward_tiles(w, fields, xs, y, n):
    centers = [fields.get(x, y, n) for x in xs]
    slopes = [deriv_x(lambda k, x=x: fields.get(x + k, y, n)) for x in xs]
    closure = closure_of(w, hidden(w, features_of(joined(centers), joined(slopes)))[3])
    result = []
    for i, x in enumerate(xs):
        moved = moved_of(fields, x, y, n, centers[i], slopes[i])
        result.append((x, centers[i], moved + closure[i * n : i * n + n]))
    return result


def shifted(value, by):
    lane = lax.broadcasted_iota(jnp.int32, value.shape, 1)
    if by > 0:
        return jnp.where(lane >= by, pltpu.roll(value, by, 1), 0.0)
    return jnp.where(lane < LEV + by, pltpu.roll(value, LEV + by, 1), 0.0)


def settle(source, fall_rate, sign):
    fresh = 1.0 / (1.0 + fall_rate)
    factor = fall_rate * fresh
    value = fresh * source
    step = 1
    while step < LEV:
        value = value + factor * shifted(value, sign * step)
        factor = factor * factor
        step *= 2
    return value


def column_terms(patch, xs, y, n, fall, live, radiation, packs, adjoint):
    p_theta, p_rain, p_fall, p_live = packs
    for i, x in enumerate(xs):
        rows = pl.ds(i * PACK, n)
        p_theta[rows, :] = patch.field(x, y, n, 3)
        p_rain[rows, :] = patch.field(x, y, n, 5)
        source = pl.ds((x + 4) * 18 + y + 5, n)
        p_fall[rows, :] = fall[source, :]
        p_live[rows, :] = live[source, :]
    size = len(xs) * PACK
    theta, rain = p_theta[0:size, :], p_rain[0:size, :]
    fall_rate, mask = p_fall[0:size, :], p_live[0:size, :]
    contract = ((1,), (0,)) if adjoint else ((1,), (1,))
    p_theta[0:size, :] = lax.dot_general(
        theta, radiation[...], (contract, ((), ())), precision=HIGHEST, preferred_element_type=F32
    )
    if adjoint:
        masked = mask * rain
        p_rain[0:size, :] = settle(masked, fall_rate, 1) - masked
    else:
        p_rain[0:size, :] = mask * (settle(rain, fall_rate, -1) - rain)


def add_columns(patch, xs, y, n, packs, gain):
    for i, x in enumerate(xs):
        patch.add_field(x, y, 3, gain * packs[0][pl.ds(i * PACK, n), :])
        patch.add_field(x, y, 5, gain * packs[1][pl.ds(i * PACK, n), :])


def backward_tiles(w, fields, lead, xs, y, n, spread, direct, sums, emit):
    centers = [fields.get(x, y, n) for x in xs]
    slopes = [deriv_x(lambda k, x=x: fields.get(x + k, y, n)) for x in xs]
    center, lam = joined(centers), joined([lead.get(x, y, n) for x in xs])
    features = features_of(center, joined(slopes))
    out_cot = to_lanes(jnp.concatenate([lam, jnp.zeros_like(lam)], axis=1).astype(BF16))
    tanh_one, hidden_one, tanh_two, hidden_two = hidden(w, features)
    pre_two = (dot(w["out_t"][...], out_cot) * (1.0 - tanh_two * tanh_two)).astype(BF16)
    pre_one = (dot(w["mid_t"][...], pre_two) * (1.0 - tanh_one * tanh_one)).astype(BF16)
    feature_cot = dot(w["in_t"][...], pre_one)
    own = to_tiles(feature_cot[0:8, :])
    other = center[:, 0:1] * lam - to_tiles(feature_cot[8:16, :])
    for i, x in enumerate(xs):
        spread.put(x, y, other[i * n : i * n + n])
        direct.put(x, y, own[i * n : i * n + n])
    if sums is None:
        return

    def kept(value):
        if n == OWN_Y:
            return value
        first = [(i * n - y) * LEV for i in range(len(xs))]
        return jnp.concatenate([value[:, k : k + OWN_Y * LEV] for k in first], axis=1)

    kept_one = kept(pre_one)
    kept_two = kept(hidden_two)
    sums[0:128, :] += dot_nt(kept(pre_two), kept(hidden_one))
    sums[128:144, :] += dot_nt(kept(features), kept_one)
    sums[144:160, :] += dot_nt(kept(out_cot), kept_two)
    if emit is not None:
        closure = closure_of(w, kept_two)
        for i, x in enumerate(xs):
            tiles = slice(-y, OWN_Y - y)
            emit(x, centers[i][tiles], slopes[i][tiles], closure[i * OWN_Y : (i + 1) * OWN_Y])


def closure_backward(
    w, fields, lead, x_lo, x_hi, y_lo, y_hi, spread, direct, sums, emit=None, own_group=2, rim_group=2
):
    n = y_hi - y_lo

    def own_x(i, carry):
        xs = [i * own_group + j for j in range(own_group)]
        backward_tiles(w, fields, lead, xs, y_lo, n, spread, direct, sums, emit)
        return carry

    def rim_x(i, carry):
        first = x_lo - 2 + i * rim_group
        first = first + (0 if first < 0 else OWN_X)
        xs = [first + j for j in range(rim_group)]
        backward_tiles(w, fields, lead, xs, y_lo, n, spread, direct, None, None)
        return carry

    repeat(OWN_X // own_group, own_x)
    repeat((x_hi - x_lo + 4 - OWN_X) // rim_group, rim_x)


def adjoint_tiles(fields, lead, x, y, n, spread, direct):
    lam = lead.get(x, y, n)
    up, down = lead.get(x, y + 1, n), lead.get(x, y - 1, n)
    s_up, s_down = fields.get(x, y + 1, n), fields.get(x, y - 1, n)
    laplace = lead.get(x + 1, y, n) + lead.get(x - 1, y, n) + up + down - 4.0 * lam
    result = deriv_x(lambda k: spread.get(x + k, y, n)) + direct.get(x, y, n) + DIFFUSION * laplace
    result = result + 0.5 * (s_up[:, 1:2] * up - s_down[:, 1:2] * down)
    along_x = deriv_x(lambda k: fields.get(x + k, y, n))
    along_y = (s_up - s_down) * 0.5
    to_u = jnp.sum(lam * along_x, axis=1, keepdims=True)
    to_v = jnp.sum(lam * along_y, axis=1, keepdims=True)
    row = lax.broadcasted_iota(jnp.int32, lam.shape, 1)
    return lam, result - jnp.where(row == 0, to_u, 0.0) - jnp.where(row == 1, to_v, 0.0)


def weights_of(bundle):
    return {
        "mid": bundle.at[0:128, :],
        "mid_t": bundle.at[128:256, :],
        "in_t": bundle.at[256:272, :],
        "out": bundle.at[272:288, :],
    }


def split_three(value):
    high = value.astype(BF16)
    rest = value - high.astype(F32)
    middle = rest.astype(BF16)
    return high, middle, (rest - middle.astype(F32)).astype(BF16)


def pick(value, chosen):
    count = value.shape[0]
    parts = dot(jnp.concatenate(split_three(value), axis=0), chosen)
    return parts[0:count] + parts[count : 2 * count] + parts[2 * count : 3 * count]


def first_table():
    table = np.zeros((GZ, LEV), np.int32)
    for block in range(GZ):
        for x in range(OWN_X):
            for y in range(18):
                table[block, x * 18 + y] = x * 64 + (8 * block - 5 + y) % 64
            for y in range(14):
                table[block, 72 + x * 14 + y] = 256 + x * 64 + (8 * block - 3 + y) % 64
    return table


def pack_kernel(table, state, cot, fall, live, out, rates, left, given):
    left[:, 0:256] = state[...].reshape(96, 256)
    left[:, 256:512] = cot[...].reshape(96, 256)
    given[...] = jnp.zeros(given.shape, F32)
    given[0:1, :] = fall[...]
    given[1:2, :] = live[...].astype(F32)
    turn = 32 * turned_half(lax.axis_index("gx"))
    place = lax.broadcasted_iota(jnp.int32, (512, LEV), 0) ^ turn
    parts = jnp.concatenate(split_three(left[...]), axis=0)
    for block in range(GZ):
        chosen = jnp.where(place == table[block : block + 1, :], 1.0, 0.0).astype(BF16)
        wide = dot(parts, chosen)
        out[block] = wide[0:96] + wide[96:192] + wide[192:288]
    mine = table[pl.ds(lax.axis_index("gz"), 1), :]
    chosen = jnp.where(place[0:256] == mine, 1.0, 0.0).astype(BF16)
    rates[...] = pick(given[...], chosen)[0:8]


def turn_kernel(got, rates, to_next, to_prev):
    for which in range(NF):
        blocks = [got[k, which * 16 : which * 16 + 16, :] for k in range(GZ)]
        turned = jnp.concatenate(blocks, axis=0).T
        to_next[which * 72 : which * 72 + 72, :] = turned[0:72]
        to_prev[which * 72 : which * 72 + 72, :] = turned[0:72]
        to_next[432 + which * 28 : 460 + which * 28, :] = turned[100:128]
        to_prev[432 + which * 28 : 460 + which * 28, :] = turned[72:100]
    to_next[600:608, :] = rates[...]
    to_prev[600:608, :] = rates[...]


def forward_kernel(
    own, before, after, bundle, w_in, w_out_t, radiation,
    state, fall, live, one, to_both, next_one, prev_one,
    two, p_theta, p_rain, p_fall, p_live,
):
    w = weights_of(bundle) | {"in": w_in, "out_t": w_out_t}
    packs = (p_theta, p_rain, p_fall, p_live)
    state[...] = jnp.zeros(state.shape, F32)
    for place, source in enumerate((before, own, after)):
        for which in range(NF):
            columns = source[which * 72 : which * 72 + 72, :]
            state[pl.ds(place * 576 + which, 72, stride=8), :] = columns
        rows = pl.ds(place * 72, 72)
        fall[rows, :] = jnp.broadcast_to(source[600:601, :], (LEV, LEV)).T[0:72]
        live[rows, :] = jnp.broadcast_to(source[601:602, :], (LEV, LEV)).T[0:72]
    s_zero = Patch(state, -4, 12, -5, 18)
    s_one = Patch(one, -2, 8, -4, 16)
    s_two = Patch(two, 0, 4, -3, 14)

    def stage_one(i, carry):
        xs = [i * GROUP_ONE - 2 + j for j in range(GROUP_ONE)]
        for x, center, total in forward_tiles(w, s_zero, xs, -4, 16):
            s_one.put(x, -4, center + STEP * total)
        return carry

    repeat(8 // GROUP_ONE, stage_one)
    xs = range(-2, 6)
    column_terms(s_zero, xs, -4, 16, fall, live, radiation, packs, False)
    add_columns(s_one, xs, -4, 16, packs, STEP)

    def stage_two(i, carry):
        xs = [i * GROUP_TWO + j for j in range(GROUP_TWO)]
        for x, center, total in forward_tiles(w, s_one, xs, -3, 14):
            s_two.put(x, -3, 0.75 * s_zero.get(x, -3, 14) + 0.25 * (center + STEP * total))
        return carry

    repeat(4 // GROUP_TWO, stage_two)
    xs = range(4)
    column_terms(s_one, xs, -3, 14, fall, live, radiation, packs, False)
    add_columns(s_two, xs, -3, 14, packs, 0.25 * STEP)
    for which in range(NF):
        to_both[which * 56 : which * 56 + 56, :] = two[pl.ds(which, 56, stride=8), :]
        for i in range(4):
            rows = pl.ds(which * 48 + i * 12, 12)
            next_one[rows, :] = s_one.field(i - 2, -2, 12, which)
            prev_one[rows, :] = s_one.field(i + 2, -2, 12, which)


def middle_kernel(
    own, before, after, cot_before, prev_cot, next_cot, cot_after,
    bundle, w_in, w_out_t, radiation, state, fall, live,
    cot_two, to_both, new_state, known, sums,
    two, lead, spread, direct, p_theta, p_rain, p_fall, p_live,
):
    w = weights_of(bundle) | {"in": w_in, "out_t": w_out_t}
    packs = (p_theta, p_rain, p_fall, p_live)
    two[...] = jnp.zeros(two.shape, F32)
    for place, source in enumerate((before, own, after)):
        for which in range(NF):
            columns = source[which * 56 : which * 56 + 56, :]
            two[pl.ds(place * 448 + which, 56, stride=8), :] = columns
    lead[...] = jnp.zeros(lead.shape, F32)
    for place, source in enumerate((cot_before, prev_cot, next_cot, cot_after)):
        for which in range(NF):
            columns = source[432 + which * 28 : 460 + which * 28, :]
            lead[pl.ds(place * 224 + which, 28, stride=8), :] = (2.0 / 3.0) * columns
    sums[...] = jnp.zeros(sums.shape, F32)
    s_zero = Patch(state, -4, 12, -5, 18)
    s_two = Patch(two, -4, 12, -3, 14)
    lam = Patch(lead, -2, 8, -3, 14)
    spread_at, direct_at = Patch(spread, -2, 8, -2, 12), Patch(direct, -2, 8, -2, 12)
    c_two = Patch(cot_two, 0, 4, -2, 12)
    new = Patch(new_state, 0, 4, 0, 8)

    def emit(x, center, along_x, closure):
        total = moved_of(s_two, x, 0, OWN_Y, center, along_x) + closure
        old = s_zero.get(x, 0, OWN_Y)
        new.put(x, 0, old * (1.0 / 3.0) + (2.0 / 3.0) * (center + STEP * total))

    closure_backward(w, s_two, lam, 0, 4, -2, 10, spread_at, direct_at, sums, emit, *GROUP_B2)
    xs = range(4)
    column_terms(s_two, xs, 0, 8, fall, live, radiation, packs, False)
    add_columns(new, xs, 0, 8, packs, (2.0 / 3.0) * STEP)

    def gather(x, carry):
        center, result = adjoint_tiles(s_two, lam, x, -2, 12, spread_at, direct_at)
        c_two.put(x, -2, center + STEP * result)
        return carry

    repeat(4, gather)
    column_terms(lam, xs, -2, 12, fall, live, radiation, packs, True)
    add_columns(c_two, xs, -2, 12, packs, STEP)
    base = Patch(known, 0, 4, 0, 8)
    for x in xs:
        base.put(x, 0, 0.5 * lam.get(x, 0, 8) + 0.75 * c_two.get(x, 0, 8))
    for which in range(NF):
        to_both[which * 48 : which * 48 + 48, :] = cot_two[pl.ds(which, 48, stride=8), :]


def last_kernel(
    own, before, after, one, one_before, one_after, bundle, w_in, w_out_t, radiation,
    state, fall, live, new_state, known, sums_two,
    out,
    wide, lead, c_one, spread, direct, spread_zero, direct_zero, grad, sums,
    p_theta, p_rain, p_fall, p_live,
):
    w = weights_of(bundle) | {"in": w_in, "out_t": w_out_t}
    packs = (p_theta, p_rain, p_fall, p_live)
    wide[...] = jnp.zeros(wide.shape, F32)
    lead[...] = jnp.zeros(lead.shape, F32)
    for which in range(NF):
        rows = slice(which * 48, which * 48 + 48)
        wide[pl.ds(which, 48, stride=8), :] = one_before[rows, :]
        wide[pl.ds(1152 + which, 48, stride=8), :] = one_after[rows, :]
        lead[pl.ds(which, 48, stride=8), :] = 0.25 * before[rows, :]
        lead[pl.ds(768 + which, 48, stride=8), :] = 0.25 * after[rows, :]
    s_own = Patch(one, -2, 8, -4, 16)
    for i in range(8):
        wide[pl.ds((i + 4) * 96, 96), :] = one[pl.ds(s_own.at(i - 2, -2), 96), :]
    lead[384:768, :] = 0.25 * own[...]
    sums[...] = sums_two[...]
    s_zero = Patch(state, -4, 12, -5, 18)
    s_one = Patch(wide, -6, 16, -2, 12)
    lam_one = Patch(lead, -4, 12, -2, 12)
    lam_zero = Patch(c_one, -2, 8, -1, 10)
    spread_at, direct_at = Patch(spread, -4, 12, -1, 10), Patch(direct, -4, 12, -1, 10)
    closure_backward(w, s_one, lam_one, -2, 6, -1, 9, spread_at, direct_at, sums, None, *GROUP_B1)

    def gather_one(i, carry):
        x = i - 2
        center, result = adjoint_tiles(s_one, lam_one, x, -1, 10, spread_at, direct_at)
        lam_zero.put(x, -1, center + STEP * result)
        return carry

    repeat(8, gather_one)
    xs = range(-2, 6)
    column_terms(lam_one, xs, -1, 10, fall, live, radiation, packs, True)
    add_columns(lam_zero, xs, -1, 10, packs, STEP)

    spread_z, direct_z = Patch(spread_zero, -2, 8, 0, 8), Patch(direct_zero, -2, 8, 0, 8)
    closure_backward(w, s_zero, lam_zero, 0, 4, 0, 8, spread_z, direct_z, sums, None, *GROUP_B0)
    base = Patch(known, 0, 4, 0, 8)
    final = Patch(grad, 0, 4, 0, 8)

    def gather_zero(x, carry):
        center, result = adjoint_tiles(s_zero, lam_zero, x, 0, 8, spread_z, direct_z)
        final.put(x, 0, base.get(x, 0, 8) + center + STEP * result)
        return carry

    repeat(4, gather_zero)
    xs = range(4)
    column_terms(lam_zero, xs, 0, 8, fall, live, radiation, packs, True)
    add_columns(final, xs, 0, 8, packs, STEP)
    for pair in range(3):
        rows = []
        for source in (new_state, grad):
            for which in (2 * pair, 2 * pair + 1):
                rows.append(source[pl.ds(which, 32, stride=8), :])
        turned = jnp.concatenate(rows, axis=0).T
        for block in range(GZ):
            out[block, pair * 16 : pair * 16 + 16, :] = turned[block * 16 : block * 16 + 16]
    for block in range(GZ):
        out[block, 48:68, :] = STEP * sums[block * CHUNK : (block + 1) * CHUNK, :]


def last_table():
    chosen = np.zeros((256, 256), np.float32)
    for block in range(GZ):
        for x in range(OWN_X):
            for y in range(OWN_Y):
                chosen[block * 32 + x * 8 + y, x * 64 + block * 8 + y] = 1.0
    return chosen


def sum_kernel(got, out):
    total = got[0, 48:68, :]
    for block in range(1, GZ):
        total = total + got[block, 48:68, :]
    for other in range(out.shape[0]):
        out[other] = total


def add_kernel(got, out):
    total = got[0]
    for other in range(1, got.shape[0]):
        total = total + got[other]
    for other in range(out.shape[0]):
        out[other] = total


def unpack_kernel(got, chosen, new_state, grad):
    turn = 4 * turned_half(lax.axis_index("gx"))
    rows = []
    for part in range(4):
        lanes = slice(part * 32, part * 32 + 32)
        rows.append(jnp.concatenate([got[k ^ turn, 0:48, lanes] for k in range(GZ)], axis=1))
    placed = pick(jnp.concatenate(rows, axis=0), chosen[...])
    for part in range(4):
        for pair in range(3):
            first = part * 48 + pair * 16
            out = (new_state, grad)[part // 2]
            out[2 * pair + part % 2] = placed[first : first + 16]


def finish_kernel(got, grad_in, grad_mid, grad_out):
    total = (got[0:GZ] + got[GZ : 2 * GZ]).reshape(GZ * CHUNK, LEV)
    grad_mid[...] = total[0:128]
    rows = [total[128:134], total[136:142], jnp.zeros((116, LEV), F32)]
    grad_in[...] = jnp.concatenate(rows, axis=0).T[:, 0:12]
    grad_out[...] = total[144:150]


def call(kernel, outs, scratch, *operands, giga=0):
    vmem = pl.BlockSpec(memory_space=pltpu.VMEM)
    return pl.pallas_call(
        kernel,
        out_shape=[jax.ShapeDtypeStruct(shape, F32) for shape in outs],
        in_specs=[vmem] * len(operands),
        out_specs=[vmem] * len(outs),
        scratch_shapes=[pltpu.VMEM(shape, F32) for shape in scratch],
        cost_estimate=pl.CostEstimate(flops=giga * 10**9, transcendentals=0, bytes_accessed=10**6)
        if giga
        else None,
        compiler_params=pltpu.CompilerParams(vmem_limit_bytes=48 << 20),
    )(*operands)


def turned_half(slab):
    return (slab // 4) % 2


def passed_along(shard, by):
    pairs = []
    for block in range(GZ):
        for slab in range(GX):
            other = (slab + by) % GX
            place = block ^ (4 * (turned_half(slab) ^ turned_half(other)))
            pairs.append((block * GX + slab, place * GX + other))
    return lax.ppermute(shard, ("gz", "gx"), pairs)


def on_device(state, state_cot, w_in, w_mid, w_out, radiation, fall_rate, active):
    packs = [(8 * PACK, LEV)] * 4
    in_wide = jnp.concatenate(
        [jnp.pad(w_in[:, :NF], ((0, 0), (0, 2))), jnp.pad(w_in[:, NF:], ((0, 0), (0, 2)))], axis=1
    )
    out_wide = jnp.pad(w_out, ((0, 10), (0, 0)))
    bundle = jnp.concatenate([w_mid, w_mid.T, in_wide.T, out_wide], axis=0)
    weights = (bundle, in_wide, out_wide.T, radiation)

    packed, rates = call(
        pack_kernel,
        [(GZ, 96, LEV), (8, LEV)],
        [(96, 512), (16, 256)],
        jnp.asarray(first_table()),
        state,
        state_cot,
        fall_rate.reshape(1, 256),
        active.reshape(1, 256),
    )
    got = lax.all_to_all(packed, "gz", 0, 0)
    own, own_prev = call(turn_kernel, [(608, LEV), (608, LEV)], [], got, rates)
    before, after = passed_along(own, 1), passed_along(own_prev, -1)
    zero, fall, live, one, two, next_one, prev_one = call(
        forward_kernel,
        [(1728, LEV), (216, LEV), (216, LEV), (1024, LEV), (336, LEV), (288, LEV), (288, LEV)],
        [(448, LEV)] + packs,
        own,
        before,
        after,
        *weights,
        giga=12,
    )
    two_before, two_after = passed_along(two, 1), passed_along(two, -1)
    one_before, one_after = passed_along(next_one, 1), passed_along(prev_one, -1)
    cot_two, to_both, new_state, known, sums = call(
        middle_kernel,
        [(384, LEV), (288, LEV), (256, LEV), (256, LEV), (GZ * CHUNK, LEV)],
        [(1344, LEV), (896, LEV), (768, LEV), (768, LEV)] + packs,
        two,
        two_before,
        two_after,
        before,
        own_prev,
        own,
        after,
        *weights,
        zero,
        fall,
        live,
        giga=11,
    )
    lead_before, lead_after = passed_along(to_both, 1), passed_along(to_both, -1)
    (sent,) = call(
        last_kernel,
        [(GZ, 68, LEV)],
        [(1536, LEV), (1152, LEV), (640, LEV), (960, LEV), (960, LEV), (512, LEV), (512, LEV)]
        + [(256, LEV), (GZ * CHUNK, LEV)]
        + packs,
        cot_two,
        lead_before,
        lead_after,
        one,
        one_before,
        one_after,
        *weights,
        zero,
        fall,
        live,
        new_state,
        known,
        sums,
        giga=20,
    )
    got = lax.all_to_all(sent, "gz", 0, 0)
    (chunks,) = call(sum_kernel, [(16, CHUNK, LEV)], [], got)
    new_state, grad_state = call(
        unpack_kernel,
        [(NF, 16, 256), (NF, 16, 256)],
        [],
        got,
        jnp.asarray(last_table(), BF16),
    )
    level = [[8 * x + 4 * half + y for x in range(4) for y in range(4)] for half in range(2)]
    line = [
        [block * GX + 8 * x + 4 * half + y for half in range(2) for block in range(GZ)]
        for x in range(4)
        for y in range(4)
    ]
    chunks = lax.all_to_all(chunks, "gx", 0, 0, axis_index_groups=level)
    (added,) = call(add_kernel, [(16, CHUNK, LEV)], [], chunks)
    totals = lax.all_to_all(added, ("gz", "gx"), 0, 0, axis_index_groups=line)
    grads = call(finish_kernel, [(128, 2 * NF), (128, LEV), (NF, LEV)], [], totals)
    return (new_state, grad_state, *grads)


def solution(mesh):
    placed = (P(None, "gz", "gx"), P(None, "gz", "gx"), P(), P(), P(), P(), P("gx"), P("gx"))
    return jax.shard_map(
        on_device,
        mesh=mesh,
        in_specs=placed,
        out_specs=(P(None, "gz", "gx"), P(None, "gz", "gx"), P(), P(), P()),
        check_vma=False,
    )
```
